128 devices in a mesh: fem: 32 (over z, y, x_lo), basis: 4 (over x_hi, core).
Axes of the slice: x: 4 (x_hi: 2, x_lo: 2; x = x_hi * 2 + x_lo), y: 4, z: 4, core: 2. Of those that a mesh axis runs over, the one named last changes fastest.
Arguments:
- newest: float32 [128, 131072], P('basis', 'fem'), may hold values from -6 to 6
- earlier: float32 [16, 128, 131072], P('basis', None, 'fem'), may hold values from -0.015625 to 0.015625
- tiles: bfloat16 [1024, 4, 128, 128], P('fem'), may hold values from -0.25 to 0.25
- tile_cols: int32 [1024, 4], P('fem'), may hold values from 0 to 1023, as said below
Outputs:
- orthogonal: float32 [128, 131072], P('basis', 'fem')
- coefficients: float32 [16, 128, 128], P('basis')
The draws below stay inside these ranges and needn't reach their ends.
Inputs may be any that keep to these rules, and one draw needn't show every extreme that they name: `tile_cols`: slot 0 of tile row t names t itself; every tile row of the rows of fem index p names only tiles from p * 32 - 2 to (p + 1) * 32 + 1; tiles may repeat in a row.
All inputs are finite; a program needn't handle non-finite values.
Results may differ from the reference program's by a relative error of at most 0.0029.
Values may be sent and summed in bfloat16 or wider, within the bound.
A program may use at most 64 MiB of HBM per device.

```python
import jax
import jax.numpy as jnp
from jax import lax

BW = 128
TILE = 128
BLOCKS = 16
KT = 4
HALO_TILES = 2
RB = 32
NTB = 1024
NROWS = 131072


def draw_tile_cols(key, part):
    row_ids = jnp.arange(NTB, dtype=jnp.int32)
    offsets = jax.random.randint(key, (NTB, KT), -HALO_TILES, RB + HALO_TILES, dtype=jnp.int32)
    anchor = row_ids // RB * RB
    columns = jnp.clip(anchor[:, None] + offsets, 0, NTB - 1)
    slot_ids = jnp.arange(KT, dtype=jnp.int32)[None, :]
    return jnp.where(slot_ids == 0, row_ids[:, None], columns).astype(jnp.int32)


def shard_levels(stream_key, extent, cuts, least, largest):
    factor_of = 1.0
    for axis_at, blocks in cuts:
        draws = jax.random.uniform(jax.random.fold_in(jax.random.fold_in(stream_key, 6), axis_at), (blocks,), jnp.float32, least / len(cuts), largest / len(cuts))
        factor_of = factor_of * jnp.repeat(jnp.exp(draws), extent[axis_at] // blocks).reshape((-1,) + (1,) * (len(extent) - 1 - axis_at))
    return factor_of


def centred(own_key, shape, width, most, cuts=(), kind=jnp.bfloat16):
    gain = shard_levels(own_key, shape, cuts, -0.22, 0.18) if cuts else 1.0
    array = jax.random.normal(own_key, shape, jnp.float32) * width * gain
    return jnp.minimum(jnp.maximum(array, -most), most).astype(kind)


def setup_inputs(seed: int = 0) -> dict:
    key_list = jax.random.split(jax.random.key(seed), 5)
    newest = centred(key_list[0], (BW, NROWS), 1.0, 6.0, ((0, 4), (1, 32)), jnp.float32)
    earlier = centred(key_list[1], (BLOCKS, BW, NROWS), NROWS ** -0.5, 0.015625, ((0, 4), (2, 32)), jnp.float32)
    tiles = centred(key_list[2], (NTB, KT, TILE, TILE), (KT * TILE) ** -0.5, 0.25, ((0, 32),))
    tile_cols = draw_tile_cols(jax.random.fold_in(key_list[4], 71), 0)
    return dict(newest=newest, earlier=earlier, tiles=tiles, tile_cols=tile_cols)


def project_out(current, earlier_rows):
    highest = lax.Precision.HIGHEST
    gram_block = lax.dot_general(earlier_rows, current, (((1,), (1,)), ((), ())), precision=highest, preferred_element_type=jnp.float32)
    removed = lax.dot_general(gram_block, earlier_rows, (((0,), (0,)), ((), ())), precision=highest, preferred_element_type=jnp.float32)
    return current - removed, gram_block


def reference(newest, earlier, tiles, tile_cols):
    highest = lax.Precision.HIGHEST
    rounded = lax.optimization_barrier(newest.astype(jnp.bfloat16)).astype(jnp.float32)
    tile_view = rounded.reshape(BW, NTB, TILE)
    picked = tile_view[:, tile_cols, :]
    image = jnp.einsum("ctkj,tkij->cti", picked, tiles.astype(jnp.float32), precision=highest)
    image = image.reshape(BW, NROWS)
    earlier_rows = earlier.reshape(BLOCKS * BW, NROWS)
    once, first = project_out(image, earlier_rows)
    twice, second = project_out(once, earlier_rows)
    return twice, (first + second).reshape(BLOCKS, BW, BW)
```

```python
import functools

import jax
import jax.numpy as jnp
from jax import lax
from jax.experimental import pallas as pl
from jax.experimental.pallas import tpu as pltpu
from jax.sharding import PartitionSpec as P

HALO = 2
MESH = pl.DeviceIdType.MESH
F32 = jnp.float32
BF16 = jnp.bfloat16
NT = (((1,), (1,)), ((), ()))
NN = (((1,), (0,)), ((), ()))


def mm(a, b, dims):
    return lax.dot_general(a, b, dims, preferred_element_type=F32)


def kernel(
    nf,
    newest, earlier, tiles, cols,
    out, coef,
    nbuf, vbuf, vh, vl, tbuf, near, far, w, fb, sec, secb,
    acc, rs1s, rs1r, red1, ag1, rs2s, rs2r, red2, ag2,
    m1s, m1r, keep, xs, xr, m2s, m2r,
    qo, qs, qr, x2s, x2r,
    ld, vsem, tsem, xsend, xrecv, asend, arecv,
    m1ss, m1rs, xss, xrs, m2ss, m2rs, qss, qrs, x2ss, x2rs,
):
    f = lax.axis_index("fem")
    b = lax.axis_index("basis")
    core = b % 2
    chip = b // 2
    mate = b + 1 - 2 * core
    across = (b + 2) % 4
    corner = (mate + 2) % 4
    nblk, tile, rows = earlier.shape
    trows = tiles.shape[0]
    ncol = 4 * newest.shape[0]
    mine = newest.shape[0]
    half = rows // 2
    nv = nblk * tile

    load_n = pltpu.make_async_copy(newest, nbuf, ld.at[0])
    load_n.start()
    load_v = [pltpu.make_async_copy(earlier.at[i], vbuf.at[i], vsem.at[i]) for i in range(nblk)]
    for c in load_v:
        c.start()
    tq = trows // 4
    load_t = [
        pltpu.make_async_copy(tiles.at[pl.ds(i * tq, tq)], tbuf.at[pl.ds(i * tq, tq)], tsem.at[i])
        for i in range(4)
    ]
    for c in load_t:
        c.start()

    barrier = pltpu.get_barrier_semaphore()

    def greet(i, _):
        pl.semaphore_signal(barrier, inc=1, device_id=((f + i) % nf, b), device_id_type=MESH)
        return 0

    lax.fori_loop(1, nf, greet, 0)
    for other in (mate, across):
        pl.semaphore_signal(barrier, inc=1, device_id=(f, other), device_id_type=MESH)

    load_n.wait()
    my_rows = pl.ds(pl.multiple_of(b * mine, mine), mine)
    lane = pl.ds(pl.multiple_of(core * mine, mine), mine)
    for t in range(trows):
        near[HALO + t, lane, :] = nbuf[:, t * tile:(t + 1) * tile].astype(BF16)
    pl.semaphore_wait(barrier, nf - 1 + 2)

    def remote(src, dst, ssem, rsem, dev):
        return pltpu.make_async_remote_copy(
            src_ref=src, dst_ref=dst, send_sem=ssem, recv_sem=rsem, device_id=dev, device_id_type=MESH
        )

    def x_part(buf, first, count):
        return buf.at[pl.ds(first, count), lane, :]

    def x_send(slot, src, dst, first, count, dev):
        return remote(x_part(src, first, count), x_part(dst, first, count), xsend.at[slot], xrecv.at[slot], dev)

    hq = trows // 2
    main = [(HALO, hq), (HALO + hq, hq)]
    ends = [(0, HALO), (HALO + trows, HALO)]
    up = remote(
        x_part(near, trows, HALO), x_part(near, 0, HALO), xsend.at[0], xrecv.at[0], ((f + 1) % nf, b)
    )
    down = remote(
        x_part(near, HALO, HALO), x_part(near, HALO + trows, HALO), xsend.at[1], xrecv.at[1], ((f + nf - 1) % nf, b)
    )
    up.start()
    down.start()
    to_across = [x_send(2 + i, near, far, s, n, (f, across)) for i, (s, n) in enumerate(main)]
    to_mate = [x_send(4 + i, near, near, s, n, (f, mate)) for i, (s, n) in enumerate(main)]
    for c in to_across + to_mate:
        c.start()

    step = 32

    def split(i):
        load_v[i].wait()

        def body(r, _):
            at = pl.ds(pl.multiple_of(r * step, step), step)
            to = pl.ds(pl.multiple_of(i * tile + r * step, step), step)
            v = vbuf[i, at, :]
            hi = v.astype(BF16)
            vh[to, :] = hi
            vl[to, :] = (v - hi.astype(F32)).astype(BF16)
            return 0

        lax.fori_loop(0, tile // step, body, 0)

    split(0)
    split(1)
    up.wait_recv()
    down.wait_recv()
    ends_across = [x_send(6 + i, near, far, s, n, (f, across)) for i, (s, n) in enumerate(ends)]
    ends_mate = [x_send(8 + i, near, near, s, n, (f, mate)) for i, (s, n) in enumerate(ends)]
    for c in ends_mate + ends_across:
        c.start()
    split(2)
    split(3)
    for c in load_t:
        c.wait()
    for c in to_mate + ends_mate:
        c.wait_recv()

    pair = 2 * mine
    base = f * trows - HALO

    def image(which, src):
        at = pl.ds(pl.multiple_of(which * pair, pair), pair)

        def body(t, _):
            lhs = jnp.concatenate([src[jnp.clip(cols[t, k] - base, 0, trows + 2 * HALO - 1)] for k in range(tiles.shape[1])], axis=1)
            rhs = jnp.concatenate([tbuf[t, k] for k in range(tiles.shape[1])], axis=1)
            w[at, pl.ds(pl.multiple_of(t * tile, tile), tile)] = mm(lhs, rhs, NT)
            return 0

        lax.fori_loop(0, trows, body, 0, unroll=2)

    image(chip, near)
    relay = []
    for i, (s, n) in enumerate(main + ends):
        (to_across + ends_across)[i].wait_recv()
        c = x_send(10 + i, far, far, s, n, (f, mate))
        c.start()
        relay.append(c)
    for c in relay:
        c.wait_recv()
    image(1 - chip, far)

    kc = 512
    nk = rows // kc
    acc[...] = jnp.zeros_like(acc)

    def gram1(k, _):
        at = pl.ds(pl.multiple_of(k * kc, kc), kc)
        acc[...] += mm(w[:, at].astype(BF16), vh[:, at], NT)
        return 0

    lax.fori_loop(0, nk, gram1, 0)

    nb, nvb = ncol // 16, nv // tile
    share = nb * nvb // nf

    def all_reduce(stage, ss, rr, red, ag):
        for i in range(nb):
            for j in range(nvb):
                ss[i * nvb + j] = acc[i * 16:(i + 1) * 16, j * tile:(j + 1) * tile].astype(ss.dtype)
        own = pl.ds(f * share, share)

        def spread(src_of, dst, sem):
            def body(i, _):
                p = (f + i) % nf
                remote(src_of(p), dst, asend.at[sem], arecv.at[sem], (p, b)).start()
                return 0

            lax.fori_loop(1, nf, body, 0)

        def bytes_of(ref, sem):
            part = ref.at[pl.ds(0, (nf - 1) * share)]
            return remote(part, part, asend.at[sem], arecv.at[sem], ((f + 1) % nf, b))

        spread(lambda p: ss.at[pl.ds(p * share, share)], rr.at[own], stage)
        rr[own] = ss[own]
        bytes_of(rr, stage).wait_recv()
        total = rr[pl.ds(0, share)].astype(F32)
        for p in range(1, nf):
            total = total + rr[pl.ds(p * share, share)].astype(F32)
        red[...] = total.astype(red.dtype)
        spread(lambda p: red, ag.at[own], stage + 1)
        ag[own] = red[...]
        bytes_of(ag, stage + 1).wait_recv()
        return bytes_of(rr, stage), bytes_of(ag, stage + 1)

    sent = list(all_reduce(0, rs1s, rs1r, red1, ag1))
    for i in range(nb):
        for j in range(nvb):
            fb[i * 16:(i + 1) * 16, j * tile:(j + 1) * tile] = ag1[i * nvb + j]

    npc = half // kc
    m1 = [remote(m1s.at[j], m1r.at[j], m1ss.at[j], m1rs.at[j], (f, mate)) for j in range(npc)]
    m2 = [remote(m2s.at[j], m2r.at[j], m2ss.at[j], m2rs.at[j], (f, mate)) for j in range(npc)]
    xx = [remote(xs.at[j], xr.at[j], xss.at[j], xrs.at[j], (f, across)) for j in range(npc)]

    def piece(side, j):
        return pl.ds(pl.multiple_of(side * half + j * kc, kc), kc)

    for j in range(npc):
        m1s[j] = mm(fb[...], vh[:, piece(1 - core, j)], NN).astype(BF16)
        m1[j].start()
    for j in range(npc):
        part = mm(fb[...], vh[:, piece(core, j)], NN)
        m1[j].wait_recv()
        part = part + m1r[j].astype(F32)
        keep[j] = part
        xs[j] = part.astype(BF16)
        xx[j].start()
    acc[...] = jnp.zeros_like(acc)

    def gram2(at, removed):
        once = w[:, at] - removed
        w[:, at] = once
        hi = once.astype(BF16)
        lo = (once - hi.astype(F32)).astype(BF16)
        two = mm(jnp.concatenate([hi, lo], axis=0), vh[:, at], NT)
        acc[...] += two[:ncol] + two[ncol:] + mm(hi, vl[:, at], NT)

    for j in range(npc):
        xx[j].wait_recv()
        removed = keep[j] + xr[j].astype(F32)
        m2s[j] = removed.astype(BF16)
        m2[j].start()
        gram2(piece(core, j), removed)
        m2[j].wait_recv()
        gram2(piece(1 - core, j), m2r[j].astype(F32))

    sent += list(all_reduce(2, rs2s, rs2r, red2, ag2))
    for i in range(nb):
        for j in range(nvb):
            sec[i * 16:(i + 1) * 16, j * tile:(j + 1) * tile] = ag2[i * nvb + j]
    secb[...] = sec[...].astype(BF16)

    qc = qo.shape[2]
    nq = rows // qc
    mq = [remote(qs.at[j], qr.at[j], qss.at[j], qrs.at[j], (f, mate)) for j in range(nq)]
    xq = [remote(x2s.at[j], x2r.at[j], x2ss.at[j], x2rs.at[j], (f, across)) for j in range(nq)]

    def rows_of(owner):
        return pl.ds(pl.multiple_of(owner * mine, mine), mine)

    for j in range(nq):
        qo[j] = mm(secb[...], vh[:, j * qc:(j + 1) * qc], NN)
        qs[j, 0:mine] = qo[j, rows_of(corner), :].astype(BF16)
        qs[j, mine:2 * mine] = qo[j, rows_of(mate), :].astype(BF16)
        mq[j].start()
    for j in range(nq):
        mq[j].wait_recv()
        x2s[j] = (qo[j, rows_of(across), :] + qr[j, 0:mine].astype(F32)).astype(BF16)
        xq[j].start()
    for i in range(nblk):
        at = slice(i * tile, (i + 1) * tile)
        coef[i] = (fb[:, at].astype(F32) + sec[:, at]).T
    for j in range(nq):
        at = slice(j * qc, (j + 1) * qc)
        xq[j].wait_recv()
        taken = qo[j, my_rows, :] + qr[j, mine:2 * mine].astype(F32) + x2r[j].astype(F32)
        out[:, at] = w[my_rows, at] - taken

    for c in [up, down] + to_across + to_mate + ends_across + ends_mate + relay + m1 + m2 + xx + mq + xq + sent:
        c.wait_send()


def shards(newest, earlier, tiles, tile_cols):
    nf = lax.axis_size("fem")
    mine, rows = newest.shape
    nblk, tile, _ = earlier.shape
    trows, kt = tile_cols.shape
    ncol = 4 * mine
    nv = nblk * tile
    blocks = (ncol // 16) * (nv // tile)
    share = blocks // nf
    kc = 512
    npc = rows // 2 // kc
    qc = 1024
    nq = rows // qc
    vm = pltpu.VMEM
    dma = lambda n: pltpu.SemaphoreType.DMA((n,))
    scratch = [
        vm((mine, rows), F32),
        vm((nblk, tile, rows), F32),
        vm((nv, rows), BF16),
        vm((nv, rows), BF16),
        vm(tiles.shape, BF16),
        vm((trows + 2 * HALO, 2 * mine, tile), BF16),
        vm((trows + 2 * HALO, 2 * mine, tile), BF16),
        vm((ncol, rows), F32),
        vm((ncol, nv), BF16),
        vm((ncol, nv), F32),
        vm((ncol, nv), BF16),
        vm((ncol, nv), F32),
        vm((blocks, 16, tile), BF16), vm((blocks, 16, tile), BF16), vm((share, 16, tile), BF16), vm((blocks, 16, tile), BF16),
        vm((blocks, 16, tile), F32), vm((blocks, 16, tile), F32), vm((share, 16, tile), F32), vm((blocks, 16, tile), F32),
        vm((npc, ncol, kc), BF16), vm((npc, ncol, kc), BF16), vm((npc, ncol, kc), F32),
        vm((npc, ncol, kc), BF16), vm((npc, ncol, kc), BF16), vm((npc, ncol, kc), BF16), vm((npc, ncol, kc), BF16),
        vm((nq, ncol, qc), F32), vm((nq, 2 * mine, qc), BF16), vm((nq, 2 * mine, qc), BF16),
        vm((nq, mine, qc), BF16), vm((nq, mine, qc), BF16),
        dma(1), dma(nblk), dma(4), dma(14), dma(14), dma(4), dma(4),
        dma(npc), dma(npc), dma(npc), dma(npc), dma(npc), dma(npc), dma(nq), dma(nq), dma(nq), dma(nq),
    ]
    anywhere = pl.BlockSpec(memory_space=pl.ANY)
    return pl.pallas_call(
        functools.partial(kernel, nf),
        out_shape=(
            jax.ShapeDtypeStruct((mine, rows), F32),
            jax.ShapeDtypeStruct((nblk, tile, ncol), F32),
        ),
        in_specs=[anywhere, anywhere, anywhere, pl.BlockSpec(memory_space=pltpu.SMEM)],
        out_specs=(pl.BlockSpec(memory_space=pltpu.VMEM), pl.BlockSpec(memory_space=pltpu.VMEM)),
        scratch_shapes=scratch,
        compiler_params=pltpu.CompilerParams(
            collective_id=0, has_side_effects=True, vmem_limit_bytes=60 << 20
        ),
    )(newest, earlier, tiles, tile_cols)


def solution(mesh):
    placed = (
        P("basis", "fem"),
        P("basis", None, "fem"),
        P("fem", None, None, None),
        P("fem", None),
    )
    return jax.shard_map(
        shards,
        mesh=mesh,
        in_specs=placed,
        out_specs=(P("basis", "fem"), P("basis", None, None)),
        check_vma=False,
    )
```

```python
import functools

import jax
import jax.numpy as jnp
from jax import lax
from jax.experimental import pallas as pl
from jax.experimental.pallas import tpu as pltpu
from jax.sharding import PartitionSpec as P

HALO = 2
GROUPS = 2
SUB = 8
PIECE = 1024
QPIECE = 2048
KC = 512
MESH = pl.DeviceIdType.MESH
F32 = jnp.float32
BF16 = jnp.bfloat16
NT = (((1,), (1,)), ((), ()))
NN = (((1,), (0,)), ((), ()))


def mm(a, b, dims):
    return lax.dot_general(a, b, dims, preferred_element_type=F32)


def kernel(
    nf,
    newest, earlier, tiles, cols,
    out, coef,
    nbuf, vbuf, vh, vl, tbuf, near, far0, far1, w, fb, secb, coeft,
    acc, rs1s, rs1r, red1, ag1, rs2s, rs2r, red2, ag2,
    m1s, m1r, keep, xs, xr, m2s, m2r,
    qo, qs, qr, x2s, x2r,
    ld, vsem, tsem, xsend, xrecv, asend, arecv,
    m1ss, m1rs, xss, xrs, m2ss, m2rs, qss, qrs, x2ss, x2rs,
):
    f = lax.axis_index("fem")
    b = lax.axis_index("basis")
    core = b % 2
    chip = b // 2
    mate = b + 1 - 2 * core
    across = (b + 2) % 4
    corner = (mate + 2) % 4
    nblk, tile, rows = earlier.shape
    trows, kt = tiles.shape[0], tiles.shape[1]
    mine = newest.shape[0]
    ncol = 4 * mine
    gm, gc = mine // GROUPS, ncol // GROUPS
    half = rows // 2
    nv = nblk * tile
    far = [far0, far1]
    groups = range(GROUPS)
    started = []

    load_n = pltpu.make_async_copy(newest, nbuf, ld.at[0])
    load_n.start()
    load_v = [pltpu.make_async_copy(earlier.at[i], vbuf.at[i], vsem.at[i]) for i in range(nblk)]
    for c in load_v:
        c.start()
    tq = trows // 4
    load_t = [
        pltpu.make_async_copy(tiles.at[pl.ds(i * tq, tq)], tbuf.at[pl.ds(i * tq, tq)], tsem.at[i])
        for i in range(4)
    ]
    for c in load_t:
        c.start()

    barrier = pltpu.get_barrier_semaphore()

    def greet(i, _):
        pl.semaphore_signal(barrier, inc=1, device_id=((f + i) % nf, b), device_id_type=MESH)
        return 0

    lax.fori_loop(1, nf, greet, 0)
    for other in (mate, across):
        pl.semaphore_signal(barrier, inc=1, device_id=(f, other), device_id_type=MESH)

    load_n.wait()
    lane = pl.ds(pl.multiple_of(core * mine, mine), mine)
    for t in range(trows):
        near[HALO + t, lane, :] = nbuf[:, t * tile:(t + 1) * tile].astype(BF16)
    pl.semaphore_wait(barrier, nf - 1 + 2)
    def go(copy):
        copy.start()
        started.append(copy)

    def remote(src, dst, ssem, rsem, dev):
        return pltpu.make_async_remote_copy(
            src_ref=src, dst_ref=dst, send_sem=ssem, recv_sem=rsem, device_id=dev, device_id_type=MESH
        )

    def x_send(slot, src, dst, first, count, dev):
        a = src.at[pl.ds(first, count), lane, :]
        return remote(a, dst.at[pl.ds(first, count), lane, :], xsend.at[slot], xrecv.at[slot], dev)

    def g_send(slot, src, g, first, count, dev):
        own = pl.ds(pl.multiple_of(core * gm, gm), gm)
        to = far[g].at[pl.ds(first, count), own, :]
        if src is None:
            a = to
        else:
            a = src.at[pl.ds(first, count), pl.ds(pl.multiple_of(core * mine + g * gm, gm), gm), :]
        return remote(a, to, xsend.at[slot], xrecv.at[slot], dev)

    up = remote(
        near.at[pl.ds(trows, HALO), lane, :], near.at[pl.ds(0, HALO), lane, :],
        xsend.at[0], xrecv.at[0], ((f + 1) % nf, b),
    )
    down = remote(
        near.at[pl.ds(HALO, HALO), lane, :], near.at[pl.ds(HALO + trows, HALO), lane, :],
        xsend.at[1], xrecv.at[1], ((f + nf - 1) % nf, b),
    )
    go(up)
    go(down)
    parts = [(HALO, trows), (0, HALO), (HALO + trows, HALO)]
    to_across = [[g_send(2 + 3 * g + i, near, g, s, n, (f, across)) for i, (s, n) in enumerate(parts)] for g in groups]
    to_mate = [x_send(8 + i, near, near, s, n, (f, mate)) for i, (s, n) in enumerate(parts)]
    for g in groups:
        go(to_across[g][0])
    go(to_mate[0])
    step = 32

    def split(i):
        load_v[i].wait()

        def body(r, _):
            at = pl.ds(pl.multiple_of(r * step, step), step)
            to = pl.ds(pl.multiple_of(i * tile + r * step, step), step)
            v = vbuf[i, at, :]
            hi = v.astype(BF16)
            vh[to, :] = hi
            vl[to, :] = (v - hi.astype(F32)).astype(BF16)
            return 0

        lax.fori_loop(0, tile // step, body, 0)

    split(0)
    split(1)
    up.wait_recv()
    down.wait_recv()
    for i in (1, 2):
        go(to_mate[i])
        for g in groups:
            go(to_across[g][i])
    split(2)
    split(3)
    for c in load_t:
        c.wait()
    for c in to_mate:
        c.wait_recv()
    base = f * trows - HALO

    def product(src, t):
        at = [jnp.clip(cols[k, t] - base, 0, trows + 2 * HALO - 1) for k in range(kt)]
        lhs = jnp.concatenate([src[i] for i in at], axis=1)
        rhs = jnp.concatenate([tbuf[t, k] for k in range(kt)], axis=1)
        return mm(lhs, rhs, NT)

    def image_near(t, _):
        to = pl.ds(pl.multiple_of(t * tile, tile), tile)
        made = product(near, t)
        for g in groups:
            for c in range(2):
                at = pl.ds(pl.multiple_of(g * gc + chip * 2 * gm + c * gm, gm), gm)
                w[at, to] = made[c * mine + g * gm:c * mine + (g + 1) * gm]
        return 0

    lax.fori_loop(0, trows, image_near, 0, unroll=2)

    nk = rows // KC
    nb, nvb = gc // SUB, nv // tile
    share = nb * nvb // nf
    z, y, xl = f // 8, (f // 2) % 4, f % 2
    hops = sorted(
        [(dz, dy, dx) for dz in range(4) for dy in range(4) for dx in range(2)][1:],
        key=lambda o: -(min(o[0], 4 - o[0]) + min(o[1], 4 - o[1]) + o[2]),
    )
    own = pl.ds(f * share, share)

    def spread(src_of, dst, sem):
        for dz, dy, dx in hops:
            p = ((z + dz) % 4) * 8 + ((y + dy) % 4) * 2 + (xl + dx) % 2
            remote(src_of(p), dst, asend.at[sem], arecv.at[sem], (p, b)).start()

    def bytes_of(ref, sem):
        part = ref.at[pl.ds(0, (nf - 1) * share)]
        return remote(part, part, asend.at[sem], arecv.at[sem], ((f + 1) % nf, b))

    def reduce_start(sem, ss, rr):
        for i in range(nb):
            for j in range(nvb):
                ss[i * nvb + j] = acc[i * SUB:(i + 1) * SUB, j * tile:(j + 1) * tile]
        spread(lambda p: ss.at[pl.ds(p * share, share)], rr.at[own], sem)
        rr[own] = ss[own]

    def gather_start(sem, rr, red, ag):
        waited = bytes_of(rr, sem)
        waited.wait_recv()
        started.append(waited)
        total = rr[pl.ds(0, share)]
        for p in range(1, nf):
            total = total + rr[pl.ds(p * share, share)]
        red[...] = total
        spread(lambda p: red, ag.at[own], sem + 1)
        ag[own] = total

    def gather_wait(sem, ag):
        waited = bytes_of(ag, sem + 1)
        waited.wait_recv()
        started.append(waited)

    relay = {}

    def first_gram(g):
        relay[g] = [g_send(11 + 3 * g + i, None, g, s, n, (f, mate)) for i, (s, n) in enumerate(parts)]
        for i in range(3):
            to_across[g][i].wait_recv()
            go(relay[g][i])
        for c in relay[g]:
            c.wait_recv()

        def image_far(t, _):
            to = pl.ds(pl.multiple_of(t * tile, tile), tile)
            at = pl.ds(pl.multiple_of(g * gc + (1 - chip) * 2 * gm, 2 * gm), 2 * gm)
            w[at, to] = product(far[g], t)
            return 0

        lax.fori_loop(0, trows, image_far, 0, unroll=2)
        acc[...] = jnp.zeros_like(acc)

        def gram1(k, _):
            at = pl.ds(pl.multiple_of(k * KC, KC), KC)
            acc[...] += mm(w[g * gc:(g + 1) * gc, at].astype(BF16), vh[:, at], NT)
            return 0

        lax.fori_loop(0, nk, gram1, 0)

    npc = half // PIECE
    m1 = [remote(m1s.at[j], m1r.at[j], m1ss.at[j], m1rs.at[j], (f, mate)) for j in range(GROUPS * npc)]
    m2 = [remote(m2s.at[j], m2r.at[j], m2ss.at[j], m2rs.at[j], (f, mate)) for j in range(GROUPS * npc)]
    xx = [remote(xs.at[j], xr.at[j], xss.at[j], xrs.at[j], (f, across)) for j in range(GROUPS * npc)]

    def piece(side, j):
        return pl.ds(pl.multiple_of(side * half + j * PIECE, PIECE), PIECE)

    def project(g):
        for i in range(nb):
            for j in range(nvb):
                fb[g, i * SUB:(i + 1) * SUB, j * tile:(j + 1) * tile] = ag1[g, i * nvb + j].astype(BF16)
        for j in range(npc):
            m1s[g * npc + j] = mm(fb[g], vh[:, piece(1 - core, j)], NN).astype(BF16)
            go(m1[g * npc + j])
        for j in range(npc):
            s = g * npc + j
            part = mm(fb[g], vh[:, piece(core, j)], NN)
            m1[s].wait_recv()
            part = part + m1r[s].astype(F32)
            keep[s] = part
            xs[s] = part.astype(BF16)
            go(xx[s])

    def second_gram(g):
        acc[...] = jnp.zeros_like(acc)
        mine_g = slice(g * gc, (g + 1) * gc)

        def gram2(at, removed):
            once = w[mine_g, at] - removed
            w[mine_g, at] = once
            hi = once.astype(BF16)
            lo = (once - hi.astype(F32)).astype(BF16)
            two = mm(jnp.concatenate([hi, lo], axis=0), vh[:, at], NT)
            acc[...] += two[:gc] + two[gc:] + mm(hi, vl[:, at], NT)

        for j in range(npc):
            s = g * npc + j
            xx[s].wait_recv()
            removed = keep[s] + xr[s].astype(F32)
            m2s[s] = removed.astype(BF16)
            go(m2[s])
            gram2(piece(core, j), removed)
            m2[s].wait_recv()
            gram2(piece(1 - core, j), m2r[s].astype(F32))

    nq = rows // QPIECE
    mq = [remote(qs.at[j], qr.at[j], qss.at[j], qrs.at[j], (f, mate)) for j in range(GROUPS * nq)]
    xq = [remote(x2s.at[j], x2r.at[j], x2ss.at[j], x2rs.at[j], (f, across)) for j in range(GROUPS * nq)]

    def rows_of(owner):
        return pl.ds(pl.multiple_of(owner * gm, gm), gm)

    def project_again(g):
        for i in range(nb):
            for j in range(nvb):
                sec = ag2[g, i * nvb + j]
                at = slice(i * SUB, (i + 1) * SUB), slice(j * tile, (j + 1) * tile)
                secb[at] = sec.astype(BF16)
                to = i * SUB // gm * mine + g * gm + i * SUB % gm
                coeft[to:to + SUB, at[1]] = fb[(g,) + at].astype(F32) + sec
        for j in range(nq):
            s = g * nq + j
            qo[s] = mm(secb[...], vh[:, j * QPIECE:(j + 1) * QPIECE], NN)
            qs[s, 0:gm] = qo[s, rows_of(corner), :].astype(BF16)
            qs[s, gm:2 * gm] = qo[s, rows_of(mate), :].astype(BF16)
            go(mq[s])
        for j in range(nq):
            s = g * nq + j
            mq[s].wait_recv()
            x2s[s] = (qo[s, rows_of(across), :] + qr[s, 0:gm].astype(F32)).astype(BF16)
            go(xq[s])

    def finish(g):
        for j in range(nq):
            s = g * nq + j
            at = slice(j * QPIECE, (j + 1) * QPIECE)
            xq[s].wait_recv()
            taken = qo[s, rows_of(b), :] + qr[s, gm:2 * gm].astype(F32) + x2r[s].astype(F32)
            out[g * gm:(g + 1) * gm, at] = w[pl.ds(pl.multiple_of(g * gc + b * gm, gm), gm), at] - taken

    for g in groups:
        first_gram(g)
        reduce_start(4 * g, rs1s.at[g], rs1r.at[g])
    for g in groups:
        gather_start(4 * g, rs1r.at[g], red1.at[g], ag1.at[g])
    for g in groups:
        gather_wait(4 * g, ag1.at[g])
        project(g)
    for g in groups:
        second_gram(g)
        reduce_start(4 * g + 2, rs2s.at[g], rs2r.at[g])
    for g in groups:
        gather_start(4 * g + 2, rs2r.at[g], red2.at[g], ag2.at[g])
    for g in groups:
        gather_wait(4 * g + 2, ag2.at[g])
        project_again(g)
    for i in range(nblk):
        coef[i] = coeft[:, i * tile:(i + 1) * tile].T
    for g in groups:
        finish(g)
    for c in started:
        c.wait_send()


def hand_over(a, b, a_out, b_out, sem):
    copies = [pltpu.make_async_copy(a, a_out, sem.at[0]), pltpu.make_async_copy(b, b_out, sem.at[1])]
    for c in copies:
        c.start()
    for c in copies:
        c.wait()


def shards(newest, earlier, tiles, tile_cols):
    nf = lax.axis_size("fem")
    mine, rows = newest.shape
    nblk, tile, _ = earlier.shape
    trows, kt = tile_cols.shape
    ncol = 4 * mine
    gm, gc = mine // GROUPS, ncol // GROUPS
    nv = nblk * tile
    blocks = (gc // SUB) * (nv // tile)
    share = blocks // nf
    npc = GROUPS * (rows // 2 // PIECE)
    nq = GROUPS * (rows // QPIECE)
    vm = pltpu.VMEM
    dma = lambda n: pltpu.SemaphoreType.DMA((n,))
    all_blocks = vm((GROUPS, blocks, SUB, tile), F32)
    one_share = vm((GROUPS, share, SUB, tile), F32)
    cross = vm((npc, gc, PIECE), BF16)
    ext = trows + 2 * HALO
    scratch = [
        vm((mine, rows), F32),
        vm((nblk, tile, rows), F32),
        vm((nv, rows), BF16),
        vm((nv, rows), BF16),
        vm(tiles.shape, BF16),
        vm((ext, 2 * mine, tile), BF16),
        vm((ext, 2 * gm, tile), BF16),
        vm((ext, 2 * gm, tile), BF16),
        vm((ncol, rows), F32),
        vm((GROUPS, gc, nv), BF16),
        vm((gc, nv), BF16),
        vm((ncol, nv), F32),
        vm((gc, nv), F32),
        all_blocks, all_blocks, one_share, all_blocks,
        all_blocks, all_blocks, one_share, all_blocks,
        cross, cross, vm((npc, gc, PIECE), F32),
        cross, cross, cross, cross,
        vm((nq, gc, QPIECE), F32), vm((nq, 2 * gm, QPIECE), BF16), vm((nq, 2 * gm, QPIECE), BF16),
        vm((nq, gm, QPIECE), BF16), vm((nq, gm, QPIECE), BF16),
        dma(1), dma(nblk), dma(4), dma(17), dma(17), dma(4 * GROUPS), dma(4 * GROUPS),
        dma(npc), dma(npc), dma(npc), dma(npc), dma(npc), dma(npc), dma(nq), dma(nq), dma(nq), dma(nq),
    ]
    anywhere = pl.BlockSpec(memory_space=pl.ANY)
    made = (
        jax.ShapeDtypeStruct((mine, rows), F32),
        jax.ShapeDtypeStruct((nblk, tile, ncol), F32),
    )
    done = pl.pallas_call(
        functools.partial(kernel, nf),
        out_shape=made,
        in_specs=[anywhere, anywhere, anywhere, pl.BlockSpec(memory_space=pltpu.SMEM)],
        out_specs=(pl.BlockSpec(memory_space=pltpu.VMEM), pl.BlockSpec(memory_space=pltpu.VMEM)),
        scratch_shapes=scratch,
        compiler_params=pltpu.CompilerParams(
            collective_id=0, has_side_effects=True, vmem_limit_bytes=60 << 20
        ),
    )(newest, earlier, tiles, tile_cols.T)
    return pl.pallas_call(
        hand_over,
        out_shape=made,
        in_specs=[anywhere, anywhere],
        out_specs=(anywhere, anywhere),
        scratch_shapes=[pltpu.SemaphoreType.DMA((2,))],
    )(*done)


def solution(mesh):
    placed = (
        P("basis", "fem"),
        P("basis", None, "fem"),
        P("fem", None, None, None),
        P("fem", None),
    )
    return jax.shard_map(
        shards,
        mesh=mesh,
        in_specs=placed,
        out_specs=(P("basis", "fem"), P("basis", None, None)),
        check_vma=False,
    )
```

```python
import functools

import jax
import jax.numpy as jnp
from jax import lax
from jax.experimental import pallas as pl
from jax.experimental.pallas import tpu as pltpu
from jax.sharding import PartitionSpec as P

HALO = 2
SUB = 8
PIECE = 512
QPIECE = 1024
KC = 512
MESH = pl.DeviceIdType.MESH
F32 = jnp.float32
BF16 = jnp.bfloat16
NT = (((1,), (1,)), ((), ()))
NN = (((1,), (0,)), ((), ()))


def mm(a, b, dims):
    return lax.dot_general(a, b, dims, preferred_element_type=F32)


def kernel(
    nf,
    newest, earlier, tiles, cols,
    out, coef,
    nbuf, vbuf, vh, vl, tbuf, near, far, w, fb, secb, coeft,
    acc, accg, rs1s, rs1r, red1, ag1, rs2s, rs2r, red2, ag2,
    m1s, m1r, keep, xs, xr, m2s, m2r,
    qo, qs, qr, x2s, x2r,
    ld, vsem, tsem, xsend, xrecv, asend, arecv,
    m1ss, m1rs, xss, xrs, m2ss, m2rs, qss, qrs, x2ss, x2rs,
):
    f = lax.axis_index("fem")
    b = lax.axis_index("basis")
    core = b % 2
    chip = b // 2
    mate = b + 1 - 2 * core
    across = (b + 2) % 4
    nblk, tile, rows = earlier.shape
    trows, kt = tiles.shape[0], tiles.shape[1]
    mine = newest.shape[0]
    pair = 2 * mine
    ncol = 4 * mine
    half = rows // 2
    nv = nblk * tile
    started = []

    load_n = pltpu.make_async_copy(newest, nbuf, ld.at[0])
    load_n.start()
    load_v = [pltpu.make_async_copy(earlier.at[i], vbuf.at[i], vsem.at[i]) for i in range(nblk)]
    for c in load_v:
        c.start()
    tq = trows // 4
    load_t = [
        pltpu.make_async_copy(tiles.at[pl.ds(i * tq, tq)], tbuf.at[pl.ds(i * tq, tq)], tsem.at[i])
        for i in range(4)
    ]
    for c in load_t:
        c.start()

    barrier = pltpu.get_barrier_semaphore()

    def greet(i, _):
        pl.semaphore_signal(barrier, inc=1, device_id=((f + i) % nf, b), device_id_type=MESH)
        return 0

    lax.fori_loop(1, nf, greet, 0)
    for other in (mate, across):
        pl.semaphore_signal(barrier, inc=1, device_id=(f, other), device_id_type=MESH)

    load_n.wait()
    lane = pl.ds(pl.multiple_of(core * mine, mine), mine)
    lane_mate = pl.ds(pl.multiple_of((1 - core) * mine, mine), mine)
    lane_across = pl.ds(pl.multiple_of(pair + core * mine, mine), mine)
    lane_corner = pl.ds(pl.multiple_of(pair + (1 - core) * mine, mine), mine)
    for t in range(trows):
        near[HALO + t, lane, :] = nbuf[:, t * tile:(t + 1) * tile].astype(BF16)
    pl.semaphore_wait(barrier, nf - 1 + 2)
    def go(copy):
        copy.start()
        started.append(copy)

    def remote(src, dst, ssem, rsem, dev):
        return pltpu.make_async_remote_copy(
            src_ref=src, dst_ref=dst, send_sem=ssem, recv_sem=rsem, device_id=dev, device_id_type=MESH
        )

    def x_send(slot, src, dst, first, count, dev):
        a = src.at[pl.ds(first, count), lane, :]
        return remote(a, dst.at[pl.ds(first, count), lane, :], xsend.at[slot], xrecv.at[slot], dev)

    up = remote(
        near.at[pl.ds(trows, HALO), lane, :], near.at[pl.ds(0, HALO), lane, :],
        xsend.at[0], xrecv.at[0], ((f + 1) % nf, b),
    )
    down = remote(
        near.at[pl.ds(HALO, HALO), lane, :], near.at[pl.ds(HALO + trows, HALO), lane, :],
        xsend.at[1], xrecv.at[1], ((f + nf - 1) % nf, b),
    )
    go(up)
    go(down)
    parts = [(HALO + i * tq, tq) for i in range(4)] + [(0, HALO), (HALO + trows, HALO)]
    np = len(parts)
    to_across = [x_send(2 + i, near, far, s, n, (f, across)) for i, (s, n) in enumerate(parts)]
    to_mate = [x_send(2 + np + i, near, near, s, n, (f, mate)) for i, (s, n) in enumerate(parts)]
    relay = [x_send(2 + 2 * np + i, far, far, s, n, (f, mate)) for i, (s, n) in enumerate(parts)]
    for i in range(4):
        go(to_across[i])
        go(to_mate[i])
    step = 32

    def split(i):
        load_v[i].wait()

        def body(r, _):
            at = pl.ds(pl.multiple_of(r * step, step), step)
            to = pl.ds(pl.multiple_of(i * tile + r * step, step), step)
            vh[to, :] = vbuf[i, at, :].astype(BF16)
            return 0

        lax.fori_loop(0, tile // step, body, 0)

    def split_rest(i):
        def body(r, _):
            at = pl.ds(pl.multiple_of(r * step, step), step)
            to = pl.ds(pl.multiple_of(i * tile + r * step, step), step)
            vl[to, :] = (vbuf[i, at, :] - vh[to, :].astype(F32)).astype(BF16)
            return 0

        lax.fori_loop(0, tile // step, body, 0)

    split(0)
    split(1)
    up.wait_recv()
    down.wait_recv()
    for i in (4, 5):
        go(to_mate[i])
        go(to_across[i])
    split(2)
    split(3)
    for c in load_t:
        c.wait()
    for c in to_mate:
        c.wait_recv()
    base = f * trows - HALO

    def image(src, g):
        def body(t, _):
            at = [jnp.clip(cols[k, t] - base, 0, trows + 2 * HALO - 1) for k in range(kt)]
            lhs = jnp.concatenate([src[i] for i in at], axis=1)
            rhs = jnp.concatenate([tbuf[t, k] for k in range(kt)], axis=1)
            w[g * pair:(g + 1) * pair, pl.ds(pl.multiple_of(t * tile, tile), tile)] = mm(lhs, rhs, NT)
            return 0

        lax.fori_loop(0, trows, body, 0, unroll=2)

    nk = rows // KC
    nvb = nv // tile
    z, y, xl = f // 8, (f // 2) % 4, f % 2
    hops = sorted(
        [(dz, dy, dx) for dz in range(4) for dy in range(4) for dx in range(2)][1:],
        key=lambda o: -(min(o[0], 4 - o[0]) + min(o[1], 4 - o[1]) + o[2]),
    )

    def spread(src_of, dst, sem):
        for dz, dy, dx in hops:
            p = ((z + dz) % 4) * 8 + ((y + dy) % 4) * 2 + (xl + dx) % 2
            remote(src_of(p), dst, asend.at[sem], arecv.at[sem], (p, b)).start()

    def bytes_of(ref, sem):
        part = ref.at[pl.ds(0, (nf - 1) * (ref.shape[0] // nf))]
        return remote(part, part, asend.at[sem], arecv.at[sem], ((f + 1) % nf, b))

    def reduce_start(sem, total, ss, rr):
        share = ss.shape[0] // nf
        for i in range(ss.shape[0] // nvb):
            for j in range(nvb):
                ss[i * nvb + j] = total[i * SUB:(i + 1) * SUB, j * tile:(j + 1) * tile]
        own = pl.ds(f * share, share)
        spread(lambda p: ss.at[pl.ds(p * share, share)], rr.at[own], sem)
        rr[own] = ss[own]

    def gather_start(sem, rr, red, ag):
        share = rr.shape[0] // nf
        waited = bytes_of(rr, sem)
        waited.wait_recv()
        started.append(waited)
        total = rr[pl.ds(0, share)]
        for p in range(1, nf):
            total = total + rr[pl.ds(p * share, share)]
        red[...] = total
        own = pl.ds(f * share, share)
        spread(lambda p: red, ag.at[own], sem + 1)
        ag[own] = total

    def gather_wait(sem, ag):
        waited = bytes_of(ag, sem + 1)
        waited.wait_recv()
        started.append(waited)

    def first_gram(g):
        accg[...] = jnp.zeros_like(accg)

        def body(k, _):
            at = pl.ds(pl.multiple_of(k * KC, KC), KC)
            accg[...] += mm(w[g * pair:(g + 1) * pair, at].astype(BF16), vh[:, at], NT)
            return 0

        lax.fori_loop(0, nk, body, 0)

    npc = half // PIECE
    m1 = [remote(m1s.at[j], m1r.at[j], m1ss.at[j], m1rs.at[j], (f, mate)) for j in range(2 * npc)]
    xx = [remote(xs.at[j], xr.at[j], xss.at[j], xrs.at[j], (f, across)) for j in range(2 * npc)]
    m2 = [remote(m2s.at[j], m2r.at[j], m2ss.at[j], m2rs.at[j], (f, mate)) for j in range(npc)]

    def piece(side, j):
        return pl.ds(pl.multiple_of(side * half + j * PIECE, PIECE), PIECE)

    def project(g):
        mine_g = slice(g * pair, (g + 1) * pair)
        for i in range(pair // SUB):
            for j in range(nvb):
                at = slice(g * pair + i * SUB, g * pair + (i + 1) * SUB), slice(j * tile, (j + 1) * tile)
                fb[at] = ag1[g, i * nvb + j].astype(BF16)
        for j in range(npc):
            m1s[g * npc + j] = mm(fb[mine_g], vh[:, piece(1 - core, j)], NN).astype(BF16)
            go(m1[g * npc + j])
        for j in range(npc):
            s = g * npc + j
            part = mm(fb[mine_g], vh[:, piece(core, j)], NN)
            m1[s].wait_recv()
            part = part + m1r[s].astype(F32)
            keep[s] = part
            xs[s] = part.astype(BF16)
            go(xx[s])

    def gram2(at, removed):
        once = w[:, at] - removed
        w[:, at] = once
        hi = once.astype(BF16)
        lo = (once - hi.astype(F32)).astype(BF16)
        two = mm(jnp.concatenate([hi, lo], axis=0), vh[:, at], NT)
        acc[...] += two[:ncol] + two[ncol:] + mm(hi, vl[:, at], NT)

    image(near, 0)
    first_gram(0)
    reduce_start(0, accg, rs1s.at[0], rs1r.at[0])
    for i in range(np):
        to_across[i].wait_recv()
        go(relay[i])
    for c in relay:
        c.wait_recv()
    image(far, 1)
    gather_start(0, rs1r.at[0], red1.at[0], ag1.at[0])
    first_gram(1)
    reduce_start(2, accg, rs1s.at[1], rs1r.at[1])
    acc[...] = jnp.zeros_like(acc)
    for i in range(nblk):
        split_rest(i)
    gather_start(2, rs1r.at[1], red1.at[1], ag1.at[1])
    gather_wait(0, ag1.at[0])
    project(0)
    gather_wait(2, ag1.at[1])
    project(1)
    for j in range(npc):
        xx[j].wait_recv()
        xx[npc + j].wait_recv()
        removed = jnp.concatenate(
            [keep[j] + xr[npc + j].astype(F32), keep[npc + j] + xr[j].astype(F32)], axis=0
        )
        m2s[j] = removed.astype(BF16)
        go(m2[j])
        gram2(piece(core, j), removed)
        m2[j].wait_recv()
        gram2(piece(1 - core, j), m2r[j].astype(F32))
    reduce_start(4, acc, rs2s, rs2r)
    gather_start(4, rs2r, red2, ag2)
    gather_wait(4, ag2)
    for i in range(ncol // SUB):
        for j in range(nvb):
            at = slice(i * SUB, (i + 1) * SUB), slice(j * tile, (j + 1) * tile)
            secb[at] = ag2[i * nvb + j].astype(BF16)
    nq = rows // QPIECE
    mq = [remote(qs.at[j], qr.at[j], qss.at[j], qrs.at[j], (f, mate)) for j in range(nq)]
    xq = [remote(x2s.at[j], x2r.at[j], x2ss.at[j], x2rs.at[j], (f, across)) for j in range(nq)]
    for j in range(nq):
        qo[j] = mm(secb[...], vh[:, j * QPIECE:(j + 1) * QPIECE], NN)
        qs[j, 0:mine] = qo[j, lane_corner, :].astype(BF16)
        qs[j, mine:pair] = qo[j, lane_mate, :].astype(BF16)
        go(mq[j])
    for j in range(nq):
        mq[j].wait_recv()
        x2s[j] = (qo[j, lane_across, :] + qr[j, 0:mine].astype(F32)).astype(BF16)
        go(xq[j])
    for i in range(ncol // SUB):
        g = i * SUB // pair
        to = pl.ds(pl.multiple_of((chip + g - 2 * chip * g) * pair + i * SUB % pair, SUB), SUB)
        for j in range(nvb):
            at = slice(i * SUB, (i + 1) * SUB), slice(j * tile, (j + 1) * tile)
            coeft[to, at[1]] = fb[at].astype(F32) + ag2[i * nvb + j]
    for i in range(nblk):
        coef[i] = coeft[:, i * tile:(i + 1) * tile].T
    for j in range(nq):
        at = slice(j * QPIECE, (j + 1) * QPIECE)
        xq[j].wait_recv()
        taken = qo[j, lane, :] + qr[j, mine:pair].astype(F32) + x2r[j].astype(F32)
        out[:, at] = w[lane, at] - taken
    for c in started:
        c.wait_send()


def hand_over(a, b, a_out, b_out):
    a_out[...] = a[...]
    b_out[...] = b[...]


def shards(newest, earlier, tiles, tile_cols):
    nf = lax.axis_size("fem")
    mine, rows = newest.shape
    nblk, tile, _ = earlier.shape
    trows, kt = tile_cols.shape
    ncol = 4 * mine
    pair = 2 * mine
    nv = nblk * tile
    blocks = (ncol // SUB) * (nv // tile)
    npc = rows // 2 // PIECE
    nq = rows // QPIECE
    vm = pltpu.VMEM
    dma = lambda n: pltpu.SemaphoreType.DMA((n,))
    half_blocks = vm((2, blocks // 2, SUB, tile), F32)
    all_blocks = vm((blocks, SUB, tile), F32)
    cross = vm((2 * npc, pair, PIECE), BF16)
    whole = vm((npc, ncol, PIECE), BF16)
    ext = vm((trows + 2 * HALO, pair, tile), BF16)
    scratch = [
        vm((mine, rows), F32),
        vm((nblk, tile, rows), F32),
        vm((nv, rows), BF16),
        vm((nv, rows), BF16),
        vm(tiles.shape, BF16),
        ext, ext,
        vm((ncol, rows), F32),
        vm((ncol, nv), BF16),
        vm((ncol, nv), BF16),
        vm((ncol, nv), F32),
        vm((ncol, nv), F32),
        vm((pair, nv), F32),
        half_blocks, half_blocks, vm((2, blocks // 2 // nf, SUB, tile), F32), half_blocks,
        all_blocks, all_blocks, vm((blocks // nf, SUB, tile), F32), all_blocks,
        cross, cross, vm((2 * npc, pair, PIECE), F32),
        cross, cross, whole, whole,
        vm((nq, ncol, QPIECE), F32), vm((nq, pair, QPIECE), BF16), vm((nq, pair, QPIECE), BF16),
        vm((nq, mine, QPIECE), BF16), vm((nq, mine, QPIECE), BF16),
        dma(1), dma(nblk), dma(4), dma(20), dma(20), dma(6), dma(6),
        dma(2 * npc), dma(2 * npc), dma(2 * npc), dma(2 * npc), dma(npc), dma(npc),
        dma(nq), dma(nq), dma(nq), dma(nq),
    ]
    anywhere = pl.BlockSpec(memory_space=pl.ANY)
    made = (
        jax.ShapeDtypeStruct((mine, rows), F32),
        jax.ShapeDtypeStruct((nblk, tile, ncol), F32),
    )
    done = pl.pallas_call(
        functools.partial(kernel, nf),
        out_shape=made,
        in_specs=[anywhere, anywhere, anywhere, pl.BlockSpec(memory_space=pltpu.SMEM)],
        out_specs=(pl.BlockSpec(memory_space=pltpu.VMEM), pl.BlockSpec(memory_space=pltpu.VMEM)),
        scratch_shapes=scratch,
        compiler_params=pltpu.CompilerParams(
            collective_id=0, has_side_effects=True, vmem_limit_bytes=60 << 20
        ),
    )(newest, earlier, tiles, tile_cols.T)
    return pl.pallas_call(hand_over, out_shape=made)(*done)


def solution(mesh):
    placed = (
        P("basis", "fem"),
        P("basis", None, "fem"),
        P("fem", None, None, None),
        P("fem", None),
    )
    return jax.shard_map(
        shards,
        mesh=mesh,
        in_specs=placed,
        out_specs=(P("basis", "fem"), P("basis", None, None)),
        check_vma=False,
    )
```

```python
import functools

import jax
import jax.numpy as jnp
from jax import lax
from jax.experimental import pallas as pl
from jax.experimental.pallas import tpu as pltpu
from jax.sharding import PartitionSpec as P

HALO = 2
SUB = 8
PIECE = 1024
QPIECE = 1024
KC = 4096
MESH = pl.DeviceIdType.MESH
F32 = jnp.float32
BF16 = jnp.bfloat16
NT = (((1,), (1,)), ((), ()))
NN = (((1,), (0,)), ((), ()))


def mm(a, b, dims):
    return lax.dot_general(a, b, dims, preferred_element_type=F32)


def kernel(
    nf,
    newest, earlier, tiles, cols,
    out, coef,
    nbuf, vbuf, vh, vl, tbuf, near, far, w, fb, secb, coeft,
    acc, accg, rs1s, rs1r, red1, ag1, rs2s, rs2r, red2, ag2,
    m1s, m1r, keep, xs, xr, m2s, m2r,
    qo, qs, qr, x2s, x2r,
    ld, vsem, tsem, xsend, xrecv, asend, arecv,
    m1ss, m1rs, xss, xrs, m2ss, m2rs, qss, qrs, x2ss, x2rs,
):
    f = lax.axis_index("fem")
    b = lax.axis_index("basis")
    core = b % 2
    chip = b // 2
    mate = b + 1 - 2 * core
    across = (b + 2) % 4
    nblk, tile, rows = earlier.shape
    trows, kt = tiles.shape[0], tiles.shape[1]
    mine = newest.shape[0]
    pair = 2 * mine
    ncol = 4 * mine
    half = rows // 2
    nv = nblk * tile
    started = []

    load_n = pltpu.make_async_copy(newest, nbuf, ld.at[0])
    load_n.start()
    load_v = [pltpu.make_async_copy(earlier.at[i], vbuf.at[i], vsem.at[i]) for i in range(nblk)]
    for c in load_v:
        c.start()
    tq = trows // 4
    load_t = [
        pltpu.make_async_copy(tiles.at[pl.ds(i * tq, tq)], tbuf.at[pl.ds(i * tq, tq)], tsem.at[i])
        for i in range(4)
    ]
    for c in load_t:
        c.start()

    barrier = pltpu.get_barrier_semaphore()

    def greet(i, _):
        pl.semaphore_signal(barrier, inc=1, device_id=((f + i) % nf, b), device_id_type=MESH)
        return 0

    for other in (across, mate):
        pl.semaphore_signal(barrier, inc=1, device_id=(f, other), device_id_type=MESH)
    lax.fori_loop(1, nf, greet, 0)

    load_n.wait()
    lane = pl.ds(pl.multiple_of(core * mine, mine), mine)
    lane_mate = pl.ds(pl.multiple_of((1 - core) * mine, mine), mine)
    lane_across = pl.ds(pl.multiple_of(pair + core * mine, mine), mine)
    lane_corner = pl.ds(pl.multiple_of(pair + (1 - core) * mine, mine), mine)
    for t in range(trows):
        near[HALO + t, lane, :] = nbuf[:, t * tile:(t + 1) * tile].astype(BF16)
    pl.semaphore_wait(barrier, nf - 1 + 2)
    def go(copy):
        copy.start()
        started.append(copy)

    def remote(src, dst, ssem, rsem, dev):
        return pltpu.make_async_remote_copy(
            src_ref=src, dst_ref=dst, send_sem=ssem, recv_sem=rsem, device_id=dev, device_id_type=MESH
        )

    def x_send(slot, src, dst, first, count, dev):
        a = src.at[pl.ds(first, count), lane, :]
        return remote(a, dst.at[pl.ds(first, count), lane, :], xsend.at[slot], xrecv.at[slot], dev)

    up = remote(
        near.at[pl.ds(trows, HALO), lane, :], near.at[pl.ds(0, HALO), lane, :],
        xsend.at[0], xrecv.at[0], ((f + 1) % nf, b),
    )
    down = remote(
        near.at[pl.ds(HALO, HALO), lane, :], near.at[pl.ds(HALO + trows, HALO), lane, :],
        xsend.at[1], xrecv.at[1], ((f + nf - 1) % nf, b),
    )
    go(up)
    go(down)
    parts = [(HALO + i * tq, tq) for i in range(4)] + [(0, HALO), (HALO + trows, HALO)]
    np = len(parts)
    to_across = [x_send(2 + i, near, far, s, n, (f, across)) for i, (s, n) in enumerate(parts)]
    to_mate = [x_send(2 + np + i, near, near, s, n, (f, mate)) for i, (s, n) in enumerate(parts)]
    relay = [x_send(2 + 2 * np + i, far, far, s, n, (f, mate)) for i, (s, n) in enumerate(parts)]
    for i in range(4):
        go(to_across[i])
        go(to_mate[i])
    step = 32

    def split(i):
        load_v[i].wait()

        def body(r, _):
            at = pl.ds(pl.multiple_of(r * step, step), step)
            to = pl.ds(pl.multiple_of(i * tile + r * step, step), step)
            vh[to, :] = vbuf[i, at, :].astype(BF16)
            return 0

        lax.fori_loop(0, tile // step, body, 0)

    def split_rest(i):
        def body(r, _):
            at = pl.ds(pl.multiple_of(r * step, step), step)
            to = pl.ds(pl.multiple_of(i * tile + r * step, step), step)
            vl[to, :] = (vbuf[i, at, :] - vh[to, :].astype(F32)).astype(BF16)
            return 0

        lax.fori_loop(0, tile // step, body, 0)

    split(0)
    split(1)
    up.wait_recv()
    down.wait_recv()
    for i in (4, 5):
        go(to_mate[i])
        go(to_across[i])
    split(2)
    split(3)
    for c in load_t:
        c.wait()
    for c in to_mate:
        c.wait_recv()
    base = f * trows - HALO

    def image(src, g):
        def body(t, _):
            at = [jnp.clip(cols[k, t] - base, 0, trows + 2 * HALO - 1) for k in range(kt)]
            lhs = jnp.concatenate([src[i] for i in at], axis=1)
            rhs = jnp.concatenate([tbuf[t, k] for k in range(kt)], axis=1)
            w[g * pair:(g + 1) * pair, pl.ds(pl.multiple_of(t * tile, tile), tile)] = mm(lhs, rhs, NT)
            return 0

        lax.fori_loop(0, trows, body, 0, unroll=16)

    nk = rows // KC
    nvb = nv // tile
    z, y, xl = f // 8, (f // 2) % 4, f % 2
    hops = sorted(
        [(dz, dy, dx) for dz in range(4) for dy in range(4) for dx in range(2)][1:],
        key=lambda o: -(min(o[0], 4 - o[0]) + min(o[1], 4 - o[1]) + o[2]),
    )

    def spread(src_of, dst, sem):
        for dz, dy, dx in hops:
            p = ((z + dz) % 4) * 8 + ((y + dy) % 4) * 2 + (xl + dx) % 2
            remote(src_of(p), dst, asend.at[sem], arecv.at[sem], (p, b)).start()

    def bytes_of(ref, sem):
        part = ref.at[pl.ds(0, (nf - 1) * (ref.shape[0] // nf))]
        return remote(part, part, asend.at[sem], arecv.at[sem], ((f + 1) % nf, b))

    def reduce_start(sem, total, ss, rr):
        share = ss.shape[0] // nf
        for i in range(ss.shape[0] // nvb):
            for j in range(nvb):
                ss[i * nvb + j] = total[i * SUB:(i + 1) * SUB, j * tile:(j + 1) * tile]
        own = pl.ds(f * share, share)
        spread(lambda p: ss.at[pl.ds(p * share, share)], rr.at[own], sem)
        rr[own] = ss[own]

    def gather_start(sem, rr, red, ag):
        share = rr.shape[0] // nf
        waited = bytes_of(rr, sem)
        waited.wait_recv()
        started.append(waited)
        total = rr[pl.ds(0, share)]
        for p in range(1, nf):
            total = total + rr[pl.ds(p * share, share)]
        red[...] = total
        own = pl.ds(f * share, share)
        spread(lambda p: red, ag.at[own], sem + 1)
        ag[own] = total

    def gather_wait(sem, ag):
        waited = bytes_of(ag, sem + 1)
        waited.wait_recv()
        started.append(waited)

    def first_gram(g):
        accg[...] = jnp.zeros_like(accg)

        def body(k, _):
            at = pl.ds(pl.multiple_of(k * KC, KC), KC)
            accg[...] += mm(w[g * pair:(g + 1) * pair, at].astype(BF16), vh[:, at], NT)
            return 0

        lax.fori_loop(0, nk, body, 0)

    npc = half // PIECE
    m1 = [remote(m1s.at[j], m1r.at[j], m1ss.at[j], m1rs.at[j], (f, mate)) for j in range(2 * npc)]
    xx = [remote(xs.at[j], xr.at[j], xss.at[j], xrs.at[j], (f, across)) for j in range(2 * npc)]
    m2 = [remote(m2s.at[j], m2r.at[j], m2ss.at[j], m2rs.at[j], (f, mate)) for j in range(npc)]

    def piece(side, j):
        return pl.ds(pl.multiple_of(side * half + j * PIECE, PIECE), PIECE)

    def project(g):
        mine_g = slice(g * pair, (g + 1) * pair)
        for i in range(pair // SUB):
            for j in range(nvb):
                at = slice(g * pair + i * SUB, g * pair + (i + 1) * SUB), slice(j * tile, (j + 1) * tile)
                fb[at] = ag1[g, i * nvb + j].astype(BF16)
        for j in range(npc):
            m1s[g * npc + j] = mm(fb[mine_g], vh[:, piece(1 - core, j)], NN).astype(BF16)
            go(m1[g * npc + j])
        for j in range(npc):
            s = g * npc + j
            part = mm(fb[mine_g], vh[:, piece(core, j)], NN)
            m1[s].wait_recv()
            part = part + m1r[s].astype(F32)
            keep[s] = part
            xs[s] = part.astype(BF16)
            go(xx[s])

    def gram2(at, removed):
        once = w[:, at] - removed
        w[:, at] = once
        hi = once.astype(BF16)
        lo = (once - hi.astype(F32)).astype(BF16)
        two = mm(jnp.concatenate([hi, lo], axis=0), vh[:, at], NT)
        acc[...] += two[:ncol] + two[ncol:] + mm(hi, vl[:, at], NT)

    image(near, 0)
    first_gram(0)
    reduce_start(0, accg, rs1s.at[0], rs1r.at[0])
    for i in range(np):
        to_across[i].wait_recv()
        go(relay[i])
    for c in relay:
        c.wait_recv()
    image(far, 1)
    first_gram(1)
    reduce_start(2, accg, rs1s.at[1], rs1r.at[1])
    gather_start(0, rs1r.at[0], red1.at[0], ag1.at[0])
    acc[...] = jnp.zeros_like(acc)
    for i in range(nblk):
        split_rest(i)
    gather_start(2, rs1r.at[1], red1.at[1], ag1.at[1])
    gather_wait(0, ag1.at[0])
    project(0)
    gather_wait(2, ag1.at[1])
    project(1)
    for j in range(npc):
        xx[j].wait_recv()
        xx[npc + j].wait_recv()
        removed = jnp.concatenate(
            [keep[j] + xr[npc + j].astype(F32), keep[npc + j] + xr[j].astype(F32)], axis=0
        )
        m2s[j] = removed.astype(BF16)
        go(m2[j])
        gram2(piece(core, j), removed)
        m2[j].wait_recv()
        gram2(piece(1 - core, j), m2r[j].astype(F32))
    for g in (1, 0):
        reduce_start(6 - 2 * g, acc.at[pl.ds(g * pair, pair)], rs2s.at[g], rs2r.at[g])
    for g in (1, 0):
        gather_start(6 - 2 * g, rs2r.at[g], red2.at[g], ag2.at[g])
    gather_wait(4, ag2.at[1])
    nq = rows // QPIECE
    mf = [remote(qs.at[j], qr.at[j], qss.at[j], qrs.at[j], (f, mate)) for j in range(nq)]
    mn = [
        remote(qs.at[nq + j], qr.at[nq + j], qss.at[nq + j], qrs.at[nq + j], (f, mate))
        for j in range(nq)
    ]
    xq = [remote(x2s.at[j], x2r.at[j], x2ss.at[j], x2rs.at[j], (f, across)) for j in range(nq)]

    def project_again(g, give, sends):
        mine_g = slice(g * pair, (g + 1) * pair)
        for i in range(pair // SUB):
            for j in range(nvb):
                at = slice(g * pair + i * SUB, g * pair + (i + 1) * SUB), slice(j * tile, (j + 1) * tile)
                secb[at] = ag2[g, i * nvb + j].astype(BF16)
        for j in range(nq):
            qo[j, mine_g] = mm(secb[mine_g], vh[:, j * QPIECE:(j + 1) * QPIECE], NN)
            qs[(1 - g) * nq + j] = qo[j, give, :].astype(BF16)
            go(sends[j])

    project_again(1, lane_corner, mf)
    for j in range(nq):
        mf[j].wait_recv()
        x2s[j] = (qo[j, lane_across, :] + qr[j].astype(F32)).astype(BF16)
        go(xq[j])
    gather_wait(6, ag2.at[0])
    project_again(0, lane_mate, mn)
    for g in range(2):
        to = pl.multiple_of((chip + g - 2 * chip * g) * pair, pair)
        for i in range(pair // SUB):
            for j in range(nvb):
                at = slice(g * pair + i * SUB, g * pair + (i + 1) * SUB), slice(j * tile, (j + 1) * tile)
                coeft[pl.ds(to + i * SUB, SUB), at[1]] = fb[at].astype(F32) + ag2[g, i * nvb + j]
    for i in range(nblk):
        coef[i] = coeft[:, i * tile:(i + 1) * tile].T
    for j in range(nq):
        at = slice(j * QPIECE, (j + 1) * QPIECE)
        mn[j].wait_recv()
        xq[j].wait_recv()
        taken = qo[j, lane, :] + qr[nq + j].astype(F32) + x2r[j].astype(F32)
        out[:, at] = w[lane, at] - taken
    for c in started:
        c.wait_send()


def hand_over(a, b, a_out, b_out):
    a_out[...] = a[...]
    b_out[...] = b[...]


def shards(newest, earlier, tiles, tile_cols):
    nf = lax.axis_size("fem")
    mine, rows = newest.shape
    nblk, tile, _ = earlier.shape
    trows, kt = tile_cols.shape
    ncol = 4 * mine
    pair = 2 * mine
    nv = nblk * tile
    blocks = (ncol // SUB) * (nv // tile)
    npc = rows // 2 // PIECE
    nq = rows // QPIECE
    vm = pltpu.VMEM
    dma = lambda n: pltpu.SemaphoreType.DMA((n,))
    half_blocks = vm((2, blocks // 2, SUB, tile), F32)
    cross = vm((2 * npc, pair, PIECE), BF16)
    whole = vm((npc, ncol, PIECE), BF16)
    ext = vm((trows + 2 * HALO, pair, tile), BF16)
    scratch = [
        vm((mine, rows), F32),
        vm((nblk, tile, rows), F32),
        vm((nv, rows), BF16),
        vm((nv, rows), BF16),
        vm(tiles.shape, BF16),
        ext, ext,
        vm((ncol, rows), F32),
        vm((ncol, nv), BF16),
        vm((ncol, nv), BF16),
        vm((ncol, nv), F32),
        vm((ncol, nv), F32),
        vm((pair, nv), F32),
        half_blocks, half_blocks, vm((2, blocks // 2 // nf, SUB, tile), F32), half_blocks,
        half_blocks, half_blocks, vm((2, blocks // 2 // nf, SUB, tile), F32), half_blocks,
        cross, cross, vm((2 * npc, pair, PIECE), F32),
        cross, cross, whole, whole,
        vm((nq, ncol, QPIECE), F32), vm((2 * nq, mine, QPIECE), BF16), vm((2 * nq, mine, QPIECE), BF16),
        vm((nq, mine, QPIECE), BF16), vm((nq, mine, QPIECE), BF16),
        dma(1), dma(nblk), dma(4), dma(20), dma(20), dma(8), dma(8),
        dma(2 * npc), dma(2 * npc), dma(2 * npc), dma(2 * npc), dma(npc), dma(npc),
        dma(2 * nq), dma(2 * nq), dma(nq), dma(nq),
    ]
    anywhere = pl.BlockSpec(memory_space=pl.ANY)
    made = (
        jax.ShapeDtypeStruct((mine, rows), F32),
        jax.ShapeDtypeStruct((nblk, tile, ncol), F32),
    )
    done = pl.pallas_call(
        functools.partial(kernel, nf),
        out_shape=made,
        in_specs=[anywhere, anywhere, anywhere, pl.BlockSpec(memory_space=pltpu.SMEM)],
        out_specs=(pl.BlockSpec(memory_space=pltpu.VMEM), pl.BlockSpec(memory_space=pltpu.VMEM)),
        scratch_shapes=scratch,
        compiler_params=pltpu.CompilerParams(
            collective_id=0, has_side_effects=True, vmem_limit_bytes=60 << 20
        ),
    )(newest, earlier, tiles, tile_cols.T)
    return pl.pallas_call(hand_over, out_shape=made)(*done)


def solution(mesh):
    placed = (
        P("basis", "fem"),
        P("basis", None, "fem"),
        P("fem", None, None, None),
        P("fem", None),
    )
    return jax.shard_map(
        shards,
        mesh=mesh,
        in_specs=placed,
        out_specs=(P("basis", "fem"), P("basis", None, None)),
        check_vma=False,
    )
```

```python
import functools

import jax
import jax.numpy as jnp
from jax import lax
from jax.experimental import pallas as pl
from jax.experimental.pallas import tpu as pltpu
from jax.sharding import PartitionSpec as P

HALO = 2
SUB = 8
PIECE = 1024
QPIECE = 512
KC = 4096
MESH = pl.DeviceIdType.MESH
F32 = jnp.float32
BF16 = jnp.bfloat16
NT = (((1,), (1,)), ((), ()))
NN = (((1,), (0,)), ((), ()))


def mm(a, b, dims):
    return lax.dot_general(a, b, dims, preferred_element_type=F32)


def kernel(
    nf,
    newest, earlier, tiles, cols,
    out, coef,
    nbuf, vbuf, vh, vl, tbuf, near, far, w, fb, secb, coeft,
    acc, accg, rs1s, rs1r, red1, ag1, rs2s, rs2r, red2, ag2,
    m1s, m1r, keep, xs, xr, m2s, m2r,
    qo, qs, qr, x2s, x2r,
    ld, vsem, tsem, xsend, xrecv, asend, arecv,
    m1ss, m1rs, xss, xrs, m2ss, m2rs, qss, qrs, x2ss, x2rs,
):
    f = lax.axis_index("fem")
    b = lax.axis_index("basis")
    core = b % 2
    chip = b // 2
    mate = b + 1 - 2 * core
    across = (b + 2) % 4
    nblk, tile, rows = earlier.shape
    trows, kt = tiles.shape[0], tiles.shape[1]
    mine = newest.shape[0]
    pair = 2 * mine
    ncol = 4 * mine
    half = rows // 2
    nv = nblk * tile
    started = []

    load_n = pltpu.make_async_copy(newest, nbuf, ld.at[0])
    load_n.start()
    load_v = [pltpu.make_async_copy(earlier.at[i], vbuf.at[i], vsem.at[i]) for i in range(nblk)]
    for c in load_v:
        c.start()
    tq = trows // 4
    load_t = [
        pltpu.make_async_copy(tiles.at[pl.ds(i * tq, tq)], tbuf.at[pl.ds(i * tq, tq)], tsem.at[i])
        for i in range(4)
    ]
    for c in load_t:
        c.start()

    barrier = pltpu.get_barrier_semaphore()

    def greet(i, _):
        pl.semaphore_signal(barrier, inc=1, device_id=((f + i) % nf, b), device_id_type=MESH)
        return 0

    for other in (across, mate):
        pl.semaphore_signal(barrier, inc=1, device_id=(f, other), device_id_type=MESH)
    lax.fori_loop(1, nf, greet, 0)

    load_n.wait()
    lane = pl.ds(pl.multiple_of(core * mine, mine), mine)
    lane_mate = pl.ds(pl.multiple_of((1 - core) * mine, mine), mine)
    lane_across = pl.ds(pl.multiple_of(pair + core * mine, mine), mine)
    lane_corner = pl.ds(pl.multiple_of(pair + (1 - core) * mine, mine), mine)
    for t in range(trows):
        near[HALO + t, lane, :] = nbuf[:, t * tile:(t + 1) * tile].astype(BF16)
    pl.semaphore_wait(barrier, nf - 1 + 2)
    def go(copy):
        copy.start()
        started.append(copy)

    def remote(src, dst, ssem, rsem, dev):
        return pltpu.make_async_remote_copy(
            src_ref=src, dst_ref=dst, send_sem=ssem, recv_sem=rsem, device_id=dev, device_id_type=MESH
        )

    def x_send(slot, src, dst, first, count, dev):
        a = src.at[pl.ds(first, count), lane, :]
        return remote(a, dst.at[pl.ds(first, count), lane, :], xsend.at[slot], xrecv.at[slot], dev)

    up = remote(
        near.at[pl.ds(trows, HALO), lane, :], near.at[pl.ds(0, HALO), lane, :],
        xsend.at[0], xrecv.at[0], ((f + 1) % nf, b),
    )
    down = remote(
        near.at[pl.ds(HALO, HALO), lane, :], near.at[pl.ds(HALO + trows, HALO), lane, :],
        xsend.at[1], xrecv.at[1], ((f + nf - 1) % nf, b),
    )
    go(up)
    go(down)
    parts = [(HALO + i * tq, tq) for i in range(4)] + [(0, HALO), (HALO + trows, HALO)]
    np = len(parts)
    to_across = [x_send(2 + i, near, far, s, n, (f, across)) for i, (s, n) in enumerate(parts)]
    to_mate = [x_send(2 + np + i, near, near, s, n, (f, mate)) for i, (s, n) in enumerate(parts)]
    relay = [x_send(2 + 2 * np + i, far, far, s, n, (f, mate)) for i, (s, n) in enumerate(parts)]
    for i in range(4):
        go(to_across[i])
        go(to_mate[i])
    step = 32

    def split(i):
        load_v[i].wait()

        def body(r, _):
            at = pl.ds(pl.multiple_of(r * step, step), step)
            to = pl.ds(pl.multiple_of(i * tile + r * step, step), step)
            vh[to, :] = vbuf[i, at, :].astype(BF16)
            return 0

        lax.fori_loop(0, tile // step, body, 0)

    def split_rest(i):
        def body(r, _):
            at = pl.ds(pl.multiple_of(r * step, step), step)
            to = pl.ds(pl.multiple_of(i * tile + r * step, step), step)
            vl[to, :] = (vbuf[i, at, :] - vh[to, :].astype(F32)).astype(BF16)
            return 0

        lax.fori_loop(0, tile // step, body, 0)

    split(0)
    split(1)
    up.wait_recv()
    down.wait_recv()
    for i in (4, 5):
        go(to_mate[i])
        go(to_across[i])
    split(2)
    split(3)
    for c in load_t:
        c.wait()
    for c in to_mate:
        c.wait_recv()
    base = f * trows - HALO

    def image(src, g):
        def body(t, _):
            at = [jnp.clip(cols[k, t] - base, 0, trows + 2 * HALO - 1) for k in range(kt)]
            lhs = jnp.concatenate([src[i] for i in at], axis=1)
            rhs = jnp.concatenate([tbuf[t, k] for k in range(kt)], axis=1)
            w[g * pair:(g + 1) * pair, pl.ds(pl.multiple_of(t * tile, tile), tile)] = mm(lhs, rhs, NT)
            return 0

        lax.fori_loop(0, trows, body, 0, unroll=16)

    nk = rows // KC
    nvb = nv // tile
    z, y, xl = f // 8, (f // 2) % 4, f % 2
    hops = sorted(
        [(dz, dy, dx) for dz in range(4) for dy in range(4) for dx in range(2)][1:],
        key=lambda o: -(min(o[0], 4 - o[0]) + min(o[1], 4 - o[1]) + o[2]),
    )

    def spread(src_of, dst, sem):
        for dz, dy, dx in hops:
            p = ((z + dz) % 4) * 8 + ((y + dy) % 4) * 2 + (xl + dx) % 2
            remote(src_of(p), dst, asend.at[sem], arecv.at[sem], (p, b)).start()

    def bytes_of(ref, sem):
        part = ref.at[pl.ds(0, (nf - 1) * (ref.shape[0] // nf))]
        return remote(part, part, asend.at[sem], arecv.at[sem], ((f + 1) % nf, b))

    def reduce_start(sem, total, ss, rr):
        share = ss.shape[0] // nf
        for i in range(ss.shape[0] // nvb):
            for j in range(nvb):
                ss[i * nvb + j] = total[i * SUB:(i + 1) * SUB, j * tile:(j + 1) * tile]
        own = pl.ds(f * share, share)
        spread(lambda p: ss.at[pl.ds(p * share, share)], rr.at[own], sem)
        rr[own] = ss[own]

    def gather_start(sem, rr, red, ag):
        share = rr.shape[0] // nf
        waited = bytes_of(rr, sem)
        waited.wait_recv()
        started.append(waited)
        total = rr[pl.ds(0, share)]
        for p in range(1, nf):
            total = total + rr[pl.ds(p * share, share)]
        red[...] = total
        own = pl.ds(f * share, share)
        spread(lambda p: red, ag.at[own], sem + 1)
        ag[own] = total

    def gather_wait(sem, ag):
        waited = bytes_of(ag, sem + 1)
        waited.wait_recv()
        started.append(waited)

    def first_gram(g):
        accg[...] = jnp.zeros_like(accg)

        def body(k, _):
            at = pl.ds(pl.multiple_of(k * KC, KC), KC)
            accg[...] += mm(w[g * pair:(g + 1) * pair, at].astype(BF16), vh[:, at], NT)
            return 0

        lax.fori_loop(0, nk, body, 0)

    npc = half // PIECE
    m1 = [remote(m1s.at[j], m1r.at[j], m1ss.at[j], m1rs.at[j], (f, mate)) for j in range(2 * npc)]
    xx = [remote(xs.at[j], xr.at[j], xss.at[j], xrs.at[j], (f, across)) for j in range(2 * npc)]
    m2 = [remote(m2s.at[j], m2r.at[j], m2ss.at[j], m2rs.at[j], (f, mate)) for j in range(npc)]

    def piece(side, j):
        return pl.ds(pl.multiple_of(side * half + j * PIECE, PIECE), PIECE)

    def project(g):
        mine_g = slice(g * pair, (g + 1) * pair)
        for i in range(pair // SUB):
            for j in range(nvb):
                at = slice(g * pair + i * SUB, g * pair + (i + 1) * SUB), slice(j * tile, (j + 1) * tile)
                fb[at] = ag1[g, i * nvb + j].astype(BF16)
        for j in range(npc):
            m1s[g * npc + j] = mm(fb[mine_g], vh[:, piece(1 - core, j)], NN).astype(BF16)
            go(m1[g * npc + j])
        for j in range(npc):
            s = g * npc + j
            part = mm(fb[mine_g], vh[:, piece(core, j)], NN)
            m1[s].wait_recv()
            part = part + m1r[s].astype(F32)
            keep[s] = part
            xs[s] = part.astype(BF16)
            go(xx[s])

    def gram2(at, removed):
        once = w[:, at] - removed
        w[:, at] = once
        hi = once.astype(BF16)
        lo = (once - hi.astype(F32)).astype(BF16)
        two = mm(jnp.concatenate([hi, lo], axis=0), vh[:, at], NT)
        acc[...] += two[:ncol] + two[ncol:] + mm(hi, vl[:, at], NT)

    def hand_on(which):
        for i in which:
            to_across[i].wait_recv()
            go(relay[i])

    image(near, 0)
    hand_on([0])
    first_gram(0)
    hand_on([1, 2])
    reduce_start(0, accg, rs1s.at[0], rs1r.at[0])
    hand_on([3, 4, 5])
    for c in relay:
        c.wait_recv()
    image(far, 1)
    first_gram(1)
    reduce_start(2, accg, rs1s.at[1], rs1r.at[1])
    gather_start(0, rs1r.at[0], red1.at[0], ag1.at[0])
    acc[...] = jnp.zeros_like(acc)
    for i in range(nblk):
        split_rest(i)
    gather_start(2, rs1r.at[1], red1.at[1], ag1.at[1])
    gather_wait(0, ag1.at[0])
    project(0)
    gather_wait(2, ag1.at[1])
    project(1)
    for j in range(npc):
        xx[j].wait_recv()
        xx[npc + j].wait_recv()
        removed = jnp.concatenate(
            [keep[j] + xr[npc + j].astype(F32), keep[npc + j] + xr[j].astype(F32)], axis=0
        )
        m2s[j] = removed.astype(BF16)
        go(m2[j])
        gram2(piece(core, j), removed)
        m2[j].wait_recv()
        gram2(piece(1 - core, j), m2r[j].astype(F32))
    for g in (1, 0):
        reduce_start(6 - 2 * g, acc.at[pl.ds(g * pair, pair)], rs2s.at[g], rs2r.at[g])
    for g in (1, 0):
        gather_start(6 - 2 * g, rs2r.at[g], red2.at[g], ag2.at[g])
    gather_wait(4, ag2.at[1])
    nq = rows // QPIECE
    mf = [remote(qs.at[j], qr.at[j], qss.at[j], qrs.at[j], (f, mate)) for j in range(nq)]
    mn = [
        remote(qs.at[nq + j], qr.at[nq + j], qss.at[nq + j], qrs.at[nq + j], (f, mate))
        for j in range(nq)
    ]
    xq = [remote(x2s.at[j], x2r.at[j], x2ss.at[j], x2rs.at[j], (f, across)) for j in range(nq)]

    def project_again(g, give, sends):
        mine_g = slice(g * pair, (g + 1) * pair)
        for i in range(pair // SUB):
            for j in range(nvb):
                at = slice(g * pair + i * SUB, g * pair + (i + 1) * SUB), slice(j * tile, (j + 1) * tile)
                secb[at] = ag2[g, i * nvb + j].astype(BF16)
        for j in range(nq):
            qo[j, mine_g] = mm(secb[mine_g], vh[:, j * QPIECE:(j + 1) * QPIECE], NN)
            qs[(1 - g) * nq + j] = qo[j, give, :].astype(BF16)
            go(sends[j])

    project_again(1, lane_corner, mf)
    for j in range(nq):
        mf[j].wait_recv()
        x2s[j] = (qo[j, lane_across, :] + qr[j].astype(F32)).astype(BF16)
        go(xq[j])
    gather_wait(6, ag2.at[0])
    project_again(0, lane_mate, mn)
    for g in range(2):
        to = pl.multiple_of((chip + g - 2 * chip * g) * pair, pair)
        for i in range(pair // SUB):
            for j in range(nvb):
                at = slice(g * pair + i * SUB, g * pair + (i + 1) * SUB), slice(j * tile, (j + 1) * tile)
                coeft[pl.ds(to + i * SUB, SUB), at[1]] = fb[at].astype(F32) + ag2[g, i * nvb + j]
    for i in range(nblk):
        coef[i] = coeft[:, i * tile:(i + 1) * tile].T
    for j in range(nq):
        at = slice(j * QPIECE, (j + 1) * QPIECE)
        mn[j].wait_recv()
        xq[j].wait_recv()
        taken = qo[j, lane, :] + qr[nq + j].astype(F32) + x2r[j].astype(F32)
        out[:, at] = w[lane, at] - taken
    for c in started:
        c.wait_send()


def hand_over(a, b, a_out, b_out):
    a_out[...] = a[...]
    b_out[...] = b[...]


def shards(newest, earlier, tiles, tile_cols):
    nf = lax.axis_size("fem")
    mine, rows = newest.shape
    nblk, tile, _ = earlier.shape
    trows, kt = tile_cols.shape
    ncol = 4 * mine
    pair = 2 * mine
    nv = nblk * tile
    blocks = (ncol // SUB) * (nv // tile)
    npc = rows // 2 // PIECE
    nq = rows // QPIECE
    vm = pltpu.VMEM
    dma = lambda n: pltpu.SemaphoreType.DMA((n,))
    half_blocks = vm((2, blocks // 2, SUB, tile), F32)
    cross = vm((2 * npc, pair, PIECE), BF16)
    whole = vm((npc, ncol, PIECE), BF16)
    ext = vm((trows + 2 * HALO, pair, tile), BF16)
    scratch = [
        vm((mine, rows), F32),
        vm((nblk, tile, rows), F32),
        vm((nv, rows), BF16),
        vm((nv, rows), BF16),
        vm(tiles.shape, BF16),
        ext, ext,
        vm((ncol, rows), F32),
        vm((ncol, nv), BF16),
        vm((ncol, nv), BF16),
        vm((ncol, nv), F32),
        vm((ncol, nv), F32),
        vm((pair, nv), F32),
        half_blocks, half_blocks, vm((2, blocks // 2 // nf, SUB, tile), F32), half_blocks,
        half_blocks, half_blocks, vm((2, blocks // 2 // nf, SUB, tile), F32), half_blocks,
        cross, cross, vm((2 * npc, pair, PIECE), F32),
        cross, cross, whole, whole,
        vm((nq, ncol, QPIECE), F32), vm((2 * nq, mine, QPIECE), BF16), vm((2 * nq, mine, QPIECE), BF16),
        vm((nq, mine, QPIECE), BF16), vm((nq, mine, QPIECE), BF16),
        dma(1), dma(nblk), dma(4), dma(20), dma(20), dma(8), dma(8),
        dma(2 * npc), dma(2 * npc), dma(2 * npc), dma(2 * npc), dma(npc), dma(npc),
        dma(2 * nq), dma(2 * nq), dma(nq), dma(nq),
    ]
    anywhere = pl.BlockSpec(memory_space=pl.ANY)
    made = (
        jax.ShapeDtypeStruct((mine, rows), F32),
        jax.ShapeDtypeStruct((nblk, tile, ncol), F32),
    )
    done = pl.pallas_call(
        functools.partial(kernel, nf),
        out_shape=made,
        in_specs=[anywhere, anywhere, anywhere, pl.BlockSpec(memory_space=pltpu.SMEM)],
        out_specs=(pl.BlockSpec(memory_space=pltpu.VMEM), pl.BlockSpec(memory_space=pltpu.VMEM)),
        scratch_shapes=scratch,
        compiler_params=pltpu.CompilerParams(
            collective_id=0, has_side_effects=True, vmem_limit_bytes=60 << 20
        ),
    )(newest, earlier, tiles, tile_cols.T)
    return pl.pallas_call(hand_over, out_shape=made)(*done)


def solution(mesh):
    placed = (
        P("basis", "fem"),
        P("basis", None, "fem"),
        P("fem", None, None, None),
        P("fem", None),
    )
    return jax.shard_map(
        shards,
        mesh=mesh,
        in_specs=placed,
        out_specs=(P("basis", "fem"), P("basis", None, None)),
        check_vma=False,
    )
```

```python
import functools

import jax
import jax.numpy as jnp
from jax import lax
from jax.experimental import pallas as pl
from jax.experimental.pallas import tpu as pltpu
from jax.sharding import PartitionSpec as P

HALO = 2
SUB = 8
PIECE = 512
QPIECE = 512
KC = 4096
MESH = pl.DeviceIdType.MESH
F32 = jnp.float32
BF16 = jnp.bfloat16
NT = (((1,), (1,)), ((), ()))
NN = (((1,), (0,)), ((), ()))


def mm(a, b, dims):
    return lax.dot_general(a, b, dims, preferred_element_type=F32)


def kernel(
    nf,
    newest, earlier, tiles, cols,
    out, coef,
    nbuf, vbuf, vh, vl, tbuf, near, far, w, fb, secb, coeft,
    acc, accg, rs1s, rs1r, red1, ag1, rs2s, rs2r, red2, ag2,
    m1s, m1r, keep, xs, xr, m2s, m2r,
    qo, qs, qr, x2s, x2r,
    ld, vsem, tsem, xsend, xrecv, asend, arecv,
    m1ss, m1rs, xss, xrs, m2ss, m2rs, qss, qrs, x2ss, x2rs,
):
    f = lax.axis_index("fem")
    b = lax.axis_index("basis")
    core = b % 2
    chip = b // 2
    mate = b + 1 - 2 * core
    across = (b + 2) % 4
    nblk, tile, rows = earlier.shape
    trows, kt = tiles.shape[0], tiles.shape[1]
    mine = newest.shape[0]
    pair = 2 * mine
    ncol = 4 * mine
    half = rows // 2
    nv = nblk * tile
    started = []

    load_n = pltpu.make_async_copy(newest, nbuf, ld.at[0])
    load_n.start()
    load_v = [pltpu.make_async_copy(earlier.at[i], vbuf.at[i], vsem.at[i]) for i in range(nblk)]
    for c in load_v:
        c.start()
    tq = trows // 4
    load_t = [
        pltpu.make_async_copy(tiles.at[pl.ds(i * tq, tq)], tbuf.at[pl.ds(i * tq, tq)], tsem.at[i])
        for i in range(4)
    ]
    for c in load_t:
        c.start()

    barrier = pltpu.get_barrier_semaphore()

    def greet(i, _):
        pl.semaphore_signal(barrier, inc=1, device_id=((f + i) % nf, b), device_id_type=MESH)
        return 0

    for other in (across, mate):
        pl.semaphore_signal(barrier, inc=1, device_id=(f, other), device_id_type=MESH)
    lax.fori_loop(1, nf, greet, 0)

    load_n.wait()
    lane = pl.ds(pl.multiple_of(core * mine, mine), mine)
    lane_mate = pl.ds(pl.multiple_of((1 - core) * mine, mine), mine)
    lane_across = pl.ds(pl.multiple_of(pair + core * mine, mine), mine)
    lane_corner = pl.ds(pl.multiple_of(pair + (1 - core) * mine, mine), mine)
    for t in range(trows):
        near[HALO + t, lane, :] = nbuf[:, t * tile:(t + 1) * tile].astype(BF16)
    pl.semaphore_wait(barrier, nf - 1 + 2)
    def go(copy):
        copy.start()
        started.append(copy)

    def remote(src, dst, ssem, rsem, dev):
        return pltpu.make_async_remote_copy(
            src_ref=src, dst_ref=dst, send_sem=ssem, recv_sem=rsem, device_id=dev, device_id_type=MESH
        )

    def x_send(slot, src, dst, first, count, dev):
        a = src.at[pl.ds(first, count), lane, :]
        return remote(a, dst.at[pl.ds(first, count), lane, :], xsend.at[slot], xrecv.at[slot], dev)

    up = remote(
        near.at[pl.ds(trows, HALO), lane, :], near.at[pl.ds(0, HALO), lane, :],
        xsend.at[0], xrecv.at[0], ((f + 1) % nf, b),
    )
    down = remote(
        near.at[pl.ds(HALO, HALO), lane, :], near.at[pl.ds(HALO + trows, HALO), lane, :],
        xsend.at[1], xrecv.at[1], ((f + nf - 1) % nf, b),
    )
    go(up)
    go(down)
    parts = [(HALO + i * tq, tq) for i in range(4)] + [(0, HALO), (HALO + trows, HALO)]
    np = len(parts)
    to_across = [x_send(2 + i, near, far, s, n, (f, across)) for i, (s, n) in enumerate(parts)]
    to_mate = [x_send(2 + np + i, near, near, s, n, (f, mate)) for i, (s, n) in enumerate(parts)]
    relay = [x_send(2 + 2 * np + i, far, far, s, n, (f, mate)) for i, (s, n) in enumerate(parts)]
    for i in range(4):
        go(to_across[i])
        go(to_mate[i])
    step = 32

    def split(i):
        load_v[i].wait()

        def body(r, _):
            at = pl.ds(pl.multiple_of(r * step, step), step)
            to = pl.ds(pl.multiple_of(i * tile + r * step, step), step)
            vh[to, :] = vbuf[i, at, :].astype(BF16)
            return 0

        lax.fori_loop(0, tile // step, body, 0)

    def split_rest(i):
        def body(r, _):
            at = pl.ds(pl.multiple_of(r * step, step), step)
            to = pl.ds(pl.multiple_of(i * tile + r * step, step), step)
            vl[to, :] = (vbuf[i, at, :] - vh[to, :].astype(F32)).astype(BF16)
            return 0

        lax.fori_loop(0, tile // step, body, 0)

    split(0)
    split(1)
    up.wait_recv()
    down.wait_recv()
    for i in (4, 5):
        go(to_mate[i])
        go(to_across[i])
    split(2)
    split(3)
    for c in load_t:
        c.wait()
    for c in to_mate:
        c.wait_recv()
    base = f * trows - HALO

    def image(src, g):
        def body(t, _):
            at = [jnp.clip(cols[k, t] - base, 0, trows + 2 * HALO - 1) for k in range(kt)]
            lhs = jnp.concatenate([src[i] for i in at], axis=1)
            rhs = jnp.concatenate([tbuf[t, k] for k in range(kt)], axis=1)
            w[g * pair:(g + 1) * pair, pl.ds(pl.multiple_of(t * tile, tile), tile)] = mm(lhs, rhs, NT)
            return 0

        lax.fori_loop(0, trows, body, 0, unroll=16)

    nk = rows // KC
    nvb = nv // tile
    z, y, xl = f // 8, (f // 2) % 4, f % 2
    hops = sorted(
        [(dz, dy, dx) for dz in range(4) for dy in range(4) for dx in range(2)][1:],
        key=lambda o: -(min(o[0], 4 - o[0]) + min(o[1], 4 - o[1]) + o[2]),
    )

    def spread(src_of, dst, sem):
        for dz, dy, dx in hops:
            p = ((z + dz) % 4) * 8 + ((y + dy) % 4) * 2 + (xl + dx) % 2
            remote(src_of(p), dst, asend.at[sem], arecv.at[sem], (p, b)).start()

    def bytes_of(ref, sem):
        part = ref.at[pl.ds(0, (nf - 1) * (ref.shape[0] // nf))]
        return remote(part, part, asend.at[sem], arecv.at[sem], ((f + 1) % nf, b))

    def reduce_start(sem, total, ss, rr):
        share = ss.shape[0] // nf
        for i in range(ss.shape[0] // nvb):
            for j in range(nvb):
                ss[i * nvb + j] = total[i * SUB:(i + 1) * SUB, j * tile:(j + 1) * tile]
        own = pl.ds(f * share, share)
        spread(lambda p: ss.at[pl.ds(p * share, share)], rr.at[own], sem)
        rr[own] = ss[own]

    def gather_start(sem, rr, red, ag):
        share = rr.shape[0] // nf
        waited = bytes_of(rr, sem)
        waited.wait_recv()
        started.append(waited)
        total = rr[pl.ds(0, share)]
        for p in range(1, nf):
            total = total + rr[pl.ds(p * share, share)]
        red[...] = total
        own = pl.ds(f * share, share)
        spread(lambda p: red, ag.at[own], sem + 1)
        ag[own] = total

    def gather_wait(sem, ag):
        waited = bytes_of(ag, sem + 1)
        waited.wait_recv()
        started.append(waited)

    def first_gram(g):
        accg[...] = jnp.zeros_like(accg)

        def body(k, _):
            at = pl.ds(pl.multiple_of(k * KC, KC), KC)
            accg[...] += mm(w[g * pair:(g + 1) * pair, at].astype(BF16), vh[:, at], NT)
            return 0

        lax.fori_loop(0, nk, body, 0)

    npc = half // PIECE
    m1 = [remote(m1s.at[j], m1r.at[j], m1ss.at[j], m1rs.at[j], (f, mate)) for j in range(2 * npc)]
    xx = [remote(xs.at[j], xr.at[j], xss.at[j], xrs.at[j], (f, across)) for j in range(2 * npc)]
    m2 = [remote(m2s.at[j], m2r.at[j], m2ss.at[j], m2rs.at[j], (f, mate)) for j in range(npc)]

    def piece(side, j):
        return pl.ds(pl.multiple_of(side * half + j * PIECE, PIECE), PIECE)

    def project(g):
        mine_g = slice(g * pair, (g + 1) * pair)
        for i in range(pair // SUB):
            for j in range(nvb):
                at = slice(g * pair + i * SUB, g * pair + (i + 1) * SUB), slice(j * tile, (j + 1) * tile)
                fb[at] = ag1[g, i * nvb + j].astype(BF16)
        for j in range(npc):
            m1s[g * npc + j] = mm(fb[mine_g], vh[:, piece(1 - core, j)], NN).astype(BF16)
            go(m1[g * npc + j])
        for j in range(npc):
            s = g * npc + j
            part = mm(fb[mine_g], vh[:, piece(core, j)], NN)
            m1[s].wait_recv()
            part = part + m1r[s].astype(F32)
            keep[s] = part
            xs[s] = part.astype(BF16)
            go(xx[s])

    def gram2(at, removed):
        once = w[:, at] - removed
        w[:, at] = once
        hi = once.astype(BF16)
        lo = (once - hi.astype(F32)).astype(BF16)
        two = mm(jnp.concatenate([hi, lo], axis=0), vh[:, at], NT)
        acc[...] += two[:ncol] + two[ncol:] + mm(hi, vl[:, at], NT)

    def hand_on(which):
        for i in which:
            to_across[i].wait_recv()
            go(relay[i])

    image(near, 0)
    hand_on([0])
    first_gram(0)
    hand_on([1, 2])
    reduce_start(0, accg, rs1s.at[0], rs1r.at[0])
    hand_on([3, 4, 5])
    for c in relay:
        c.wait_recv()
    image(far, 1)
    first_gram(1)
    reduce_start(2, accg, rs1s.at[1], rs1r.at[1])
    gather_start(0, rs1r.at[0], red1.at[0], ag1.at[0])
    acc[...] = jnp.zeros_like(acc)
    for i in range(nblk):
        split_rest(i)
    gather_start(2, rs1r.at[1], red1.at[1], ag1.at[1])
    gather_wait(0, ag1.at[0])
    project(0)
    gather_wait(2, ag1.at[1])
    project(1)
    for j in range(npc):
        xx[j].wait_recv()
        xx[npc + j].wait_recv()
        removed = jnp.concatenate(
            [keep[j] + xr[npc + j].astype(F32), keep[npc + j] + xr[j].astype(F32)], axis=0
        )
        m2s[j] = removed.astype(BF16)
        go(m2[j])
        gram2(piece(core, j), removed)
        m2[j].wait_recv()
        gram2(piece(1 - core, j), m2r[j].astype(F32))
    for g in (1, 0):
        reduce_start(6 - 2 * g, acc.at[pl.ds(g * pair, pair)], rs2s.at[g], rs2r.at[g])
    for g in (1, 0):
        gather_start(6 - 2 * g, rs2r.at[g], red2.at[g], ag2.at[g])
    gather_wait(4, ag2.at[1])
    nq = rows // QPIECE
    mf = [remote(qs.at[j], qr.at[j], qss.at[j], qrs.at[j], (f, mate)) for j in range(nq)]
    mn = [
        remote(qs.at[nq + j], qr.at[nq + j], qss.at[nq + j], qrs.at[nq + j], (f, mate))
        for j in range(nq)
    ]
    xq = [remote(x2s.at[j], x2r.at[j], x2ss.at[j], x2rs.at[j], (f, across)) for j in range(nq)]

    def project_again(g, give, sends):
        mine_g = slice(g * pair, (g + 1) * pair)
        for i in range(pair // SUB):
            for j in range(nvb):
                at = slice(g * pair + i * SUB, g * pair + (i + 1) * SUB), slice(j * tile, (j + 1) * tile)
                secb[at] = ag2[g, i * nvb + j].astype(BF16)
        for j in range(nq):
            qo[j, mine_g] = mm(secb[mine_g], vh[:, j * QPIECE:(j + 1) * QPIECE], NN)
            qs[(1 - g) * nq + j] = qo[j, give, :].astype(BF16)
            go(sends[j])

    project_again(1, lane_corner, mf)
    for j in range(nq):
        mf[j].wait_recv()
        x2s[j] = (qo[j, lane_across, :] + qr[j].astype(F32)).astype(BF16)
        go(xq[j])
    gather_wait(6, ag2.at[0])
    project_again(0, lane_mate, mn)
    for g in range(2):
        to = pl.multiple_of((chip + g - 2 * chip * g) * pair, pair)
        for i in range(pair // SUB):
            for j in range(nvb):
                at = slice(g * pair + i * SUB, g * pair + (i + 1) * SUB), slice(j * tile, (j + 1) * tile)
                coeft[pl.ds(to + i * SUB, SUB), at[1]] = fb[at].astype(F32) + ag2[g, i * nvb + j]
    for i in range(nblk):
        coef[i] = coeft[:, i * tile:(i + 1) * tile].T
    for j in range(nq):
        at = slice(j * QPIECE, (j + 1) * QPIECE)
        mn[j].wait_recv()
        xq[j].wait_recv()
        taken = qo[j, lane, :] + qr[nq + j].astype(F32) + x2r[j].astype(F32)
        out[:, at] = w[lane, at] - taken
    for c in started:
        c.wait_send()


def hand_over(a, b, a_out, b_out):
    a_out[...] = a[...]
    b_out[...] = b[...]


def shards(newest, earlier, tiles, tile_cols):
    nf = lax.axis_size("fem")
    mine, rows = newest.shape
    nblk, tile, _ = earlier.shape
    trows, kt = tile_cols.shape
    ncol = 4 * mine
    pair = 2 * mine
    nv = nblk * tile
    blocks = (ncol // SUB) * (nv // tile)
    npc = rows // 2 // PIECE
    nq = rows // QPIECE
    vm = pltpu.VMEM
    dma = lambda n: pltpu.SemaphoreType.DMA((n,))
    half_blocks = vm((2, blocks // 2, SUB, tile), F32)
    cross = vm((2 * npc, pair, PIECE), BF16)
    whole = vm((npc, ncol, PIECE), BF16)
    ext = vm((trows + 2 * HALO, pair, tile), BF16)
    scratch = [
        vm((mine, rows), F32),
        vm((nblk, tile, rows), F32),
        vm((nv, rows), BF16),
        vm((nv, rows), BF16),
        vm(tiles.shape, BF16),
        ext, ext,
        vm((ncol, rows), F32),
        vm((ncol, nv), BF16),
        vm((ncol, nv), BF16),
        vm((ncol, nv), F32),
        vm((ncol, nv), F32),
        vm((pair, nv), F32),
        half_blocks, half_blocks, vm((2, blocks // 2 // nf, SUB, tile), F32), half_blocks,
        half_blocks, half_blocks, vm((2, blocks // 2 // nf, SUB, tile), F32), half_blocks,
        cross, cross, vm((2 * npc, pair, PIECE), F32),
        cross, cross, whole, whole,
        vm((nq, ncol, QPIECE), F32), vm((2 * nq, mine, QPIECE), BF16), vm((2 * nq, mine, QPIECE), BF16),
        vm((nq, mine, QPIECE), BF16), vm((nq, mine, QPIECE), BF16),
        dma(1), dma(nblk), dma(4), dma(20), dma(20), dma(8), dma(8),
        dma(2 * npc), dma(2 * npc), dma(2 * npc), dma(2 * npc), dma(npc), dma(npc),
        dma(2 * nq), dma(2 * nq), dma(nq), dma(nq),
    ]
    anywhere = pl.BlockSpec(memory_space=pl.ANY)
    made = (
        jax.ShapeDtypeStruct((mine, rows), F32),
        jax.ShapeDtypeStruct((nblk, tile, ncol), F32),
    )
    done = pl.pallas_call(
        functools.partial(kernel, nf),
        out_shape=made,
        in_specs=[anywhere, anywhere, anywhere, pl.BlockSpec(memory_space=pltpu.SMEM)],
        out_specs=(pl.BlockSpec(memory_space=pltpu.VMEM), pl.BlockSpec(memory_space=pltpu.VMEM)),
        scratch_shapes=scratch,
        compiler_params=pltpu.CompilerParams(
            collective_id=0, has_side_effects=True, vmem_limit_bytes=60 << 20
        ),
    )(newest, earlier, tiles, tile_cols.T)
    return pl.pallas_call(hand_over, out_shape=made)(*done)


def solution(mesh):
    placed = (
        P("basis", "fem"),
        P("basis", None, "fem"),
        P("fem", None, None, None),
        P("fem", None),
    )
    return jax.shard_map(
        shards,
        mesh=mesh,
        in_specs=placed,
        out_specs=(P("basis", "fem"), P("basis", None, None)),
        check_vma=False,
    )
```
